512 devices in a mesh: load: 8 (over y_hi, core), brick: 64 (over z, y_lo, x).
Axes of the slice: x: 4, y: 8 (y_hi: 4, y_lo: 2; y = y_hi * 2 + y_lo), z: 8, core: 2. Of those that a mesh axis runs over, the one named last changes fastest.
Arguments:
- density: float32 [768, 64, 128], P('brick'), may hold values from 0.1 to 0.95
- passive: int32 [768, 64, 128], P('brick'), may hold values from 0 to 2, as said below
- support: int32 [768, 64, 128], P('brick'), may hold values 0 or 1
- load_nodes: int32 [16, 64], P('load'), may hold values from 0 to 6291455
- load_force: float32 [16, 64], P('load'), may hold values from -6 to 6
- self_weight: float32 [16], P('load'), may hold values from 0.3 to 3
- body_force: float32 [16, 768, 64, 128], P('load', 'brick'), may hold values from -3 to 3
Outputs:
- new_density: float32 [768, 64, 128], P('brick', 'load')
- momentum: float32 [768, 64, 128], P('brick', 'load')
- displacement: float32 [16, 768, 64, 128], P('load', 'brick')
The draws below stay inside these ranges and needn't reach their ends.
Inputs may be any that keep to these rules, and one draw needn't show every extreme that they name: 0 marks a design voxel, 1 a passive void voxel, 2 a passive solid voxel.
All inputs are finite; a program needn't handle non-finite values. No bound on the sum of `support` on one device may be relied on, other than what follows from the above.
Results may differ from the reference program's by a relative error of at most 0.0001.
Values sent between devices are 32-bit elements; how exact they have to be, the bound alone decides.
A program may use at most 64 MiB of HBM per device.

```python
import math
import jax
import jax.numpy as jnp
from jax import lax

NY = 64
NZ = 128
POINTS = 64
SWEEPS = 5
DESIGN_ITERS = 2
NX = 768
LOADS = 16


def draw_passive(key, part):
    picked = jax.random.randint(key, (NX, NY, NZ), 0, 16)
    return jnp.where(picked == 0, 1, jnp.where(picked == 1, 2, 0)).astype(jnp.int32)


def touch_ends(result, key, smallest, largest):
    longest = result.shape.index(max(result.shape))
    spots = []
    for shift in (0, 1):
        where = [jax.random.randint(jax.random.fold_in(key, axis), (), 0, length) for axis, length in enumerate(result.shape)]
        where[longest] = (where[longest] + shift) % result.shape[longest]
        spots.append(tuple(where))
    return result.at[spots[0]].set(smallest).at[spots[1]].set(largest)


def steps_of(stream_key, extent, split, least, high):
    factor_of = 1.0
    for position, shards_of in split:
        draws = jax.random.uniform(jax.random.fold_in(jax.random.fold_in(stream_key, 6), position), (shards_of,), jnp.float32, least / len(split), high / len(split))
        factor_of = factor_of * jnp.repeat(jnp.exp(draws), extent[position] // shards_of).reshape((-1,) + (1,) * (len(extent) - 1 - position))
    return factor_of


def noise(stream_key, extent, spread, limit, split=(), dtype=jnp.bfloat16):
    factor_of = steps_of(stream_key, extent, split, -0.22, 0.18) if split else 1.0
    result = jax.random.normal(stream_key, extent, jnp.float32) * spread * factor_of
    return jnp.minimum(jnp.maximum(result, -limit), limit).astype(dtype)


def setup_inputs(seed: int = 0) -> dict:
    keys = jax.random.split(jax.random.key(seed), 8)
    density = jnp.clip(0.1 + 0.84999999 * jax.random.uniform(keys[0], (NX, NY, NZ), jnp.float32) ** steps_of(keys[0], (NX, NY, NZ), ((0, 64),), -0.2, 0.2), 0.1, 0.95)
    passive = draw_passive(jax.random.fold_in(keys[7], 71), 0)
    support = touch_ends((jax.random.randint(keys[2], (NX, NY, NZ), 0, 8) < 1).astype(jnp.int32), jax.random.fold_in(keys[2], 1), 0, 1)
    load_nodes = touch_ends(jax.random.randint(keys[3], (LOADS, POINTS), 0, NX * NY * NZ), jax.random.fold_in(keys[3], 1), 0, (NX * NY * NZ) - 1).astype(jnp.int32)
    load_force = noise(keys[4], (LOADS, POINTS), 1.0, 6.0, ((0, 8),), jnp.float32)
    self_weight = jnp.clip(jnp.exp(math.log(3.0) - 2.3025851 * jax.random.uniform(keys[5], (LOADS,), jnp.float32) ** steps_of(keys[5], (LOADS,), ((0, 8),), -0.2, 0.2)), 0.3, 3.0)
    body_force = noise(keys[6], (LOADS, NX, NY, NZ), 0.5, 3.0, ((0, 8), (1, 64)), jnp.float32)
    return {"density": density, "passive": passive, "support": support, "load_nodes": load_nodes, "load_force": load_force, "self_weight": self_weight, "body_force": body_force}


stiff_floor = 0.01
mass_shift = 0.1
spectrum_low = 0.05
spectrum_high = 2.0
moment_decay = 0.8
step_size = 0.1
volume_pull = 0.5
volume_target = 0.4
density_floor = 0.001


def neighbours(padded):
    return (padded[..., 2:, 1:-1, 1:-1], padded[..., :-2, 1:-1, 1:-1],
            padded[..., 1:-1, 2:, 1:-1], padded[..., 1:-1, :-2, 1:-1],
            padded[..., 1:-1, 1:-1, 2:], padded[..., 1:-1, 1:-1, :-2])


def pad_all(vector):
    return jnp.pad(vector, 1)


def passive_apply(design, passive):
    return jnp.where(passive == 1, density_floor, jnp.where(passive == 2, 1.0, design)).astype(jnp.float32)


def operate(vector, free_mask, stiffness, face_list, padded_free):
    freed = padded_free[..., 1:-1, 1:-1, 1:-1]
    accumulated = mass_shift * stiffness * freed
    for face_weight, beside in zip(face_list, neighbours(padded_free)):
        accumulated = accumulated + face_weight * (freed - beside)
    return free_mask * accumulated + (1.0 - free_mask) * vector


def chebyshev(source, free_mask, stiffness, face_list, diagonal, pad_fn):
    centre = 0.5 * (spectrum_high + spectrum_low)
    half_width = 0.5 * (spectrum_high - spectrum_low)
    ratio_one = centre / half_width
    previous = 1.0 / ratio_one
    solution = jnp.zeros_like(source)
    residual = source
    direction = residual / diagonal / centre
    for sweep_index in range(SWEEPS):
        solution = solution + direction
        if sweep_index < SWEEPS - 1:
            applied = operate(direction, free_mask, stiffness, face_list, pad_fn(free_mask * direction))
            residual = residual - applied
            current = 1.0 / (2.0 * ratio_one - previous)
            direction = (current * previous) * direction + (2.0 * current / half_width) * (residual / diagonal)
            previous = current
    return solution


def load_energy(freed, padded):
    energy = mass_shift * freed * freed
    for beside in neighbours(padded):
        energy = energy + 0.25 * (freed - beside) ** 2
    return energy


def inside_count(start_x, start_y, grid_shape, total_shape):
    along_x = start_x + lax.broadcasted_iota(jnp.int32, grid_shape, 0)
    along_y = start_y + lax.broadcasted_iota(jnp.int32, grid_shape, 1)
    along_z = lax.broadcasted_iota(jnp.int32, grid_shape, 2)
    edges = ((along_x == 0).astype(jnp.float32) + (along_x == total_shape[0] - 1).astype(jnp.float32)
             + (along_y == 0).astype(jnp.float32) + (along_y == total_shape[1] - 1).astype(jnp.float32)
             + (along_z == 0).astype(jnp.float32) + (along_z == total_shape[2] - 1).astype(jnp.float32))
    return 6.0 - edges


def filter_field(sensitivity, padded, neighbour_count):
    accumulated = 2.0 * sensitivity
    for beside in neighbours(padded):
        accumulated = accumulated + beside
    return accumulated / (2.0 + neighbour_count)


def design_step(design, momentum, passive, abs_total, density_total, total_cells):
    mean_step = abs_total / total_cells + 1e-6
    mean_density = density_total / total_cells
    moved = design - step_size * momentum / mean_step - volume_pull * (mean_density - volume_target)
    return passive_apply(jnp.clip(moved, density_floor, 1.0), passive)


def reference(density, passive, support, load_nodes, load_force, self_weight, body_force):
    free_mask = (1 - support).astype(jnp.float32)
    design = passive_apply(density, passive)
    momentum = jnp.zeros_like(design)
    total_cells = NX * NY * NZ
    neighbour_count = inside_count(0, 0, (NX, NY, NZ), (NX, NY, NZ))
    displacement = None
    for iteration in range(DESIGN_ITERS):
        stiffness = stiff_floor + (1.0 - stiff_floor) * design ** 3
        face_list = tuple(0.5 * (stiffness + beside) for beside in neighbours(pad_all(stiffness)))
        face_total = face_list[0]
        for face_weight in face_list[1:]:
            face_total = face_total + face_weight
        diagonal = free_mask * (face_total + mass_shift * stiffness) + (1.0 - free_mask)

        def one_load(carried, inputs):
            node_ids, forces, weight, spread_force = inputs
            points = jnp.zeros((NX * NY * NZ,), jnp.float32).at[node_ids].add(forces).reshape(NX, NY, NZ)
            source = free_mask * (points + weight * design + spread_force)
            solution = chebyshev(source, free_mask, stiffness, face_list, diagonal, pad_all)
            freed = free_mask * solution
            return carried + load_energy(freed, pad_all(freed)), solution

        energy, displacement = lax.scan(one_load, jnp.zeros((NX, NY, NZ), jnp.float32),
                                        (load_nodes, load_force, self_weight, body_force))
        sensitivity = -3.0 * (1.0 - stiff_floor) * design * design * energy
        filtered = filter_field(sensitivity, pad_all(sensitivity), neighbour_count)
        momentum = moment_decay * momentum + filtered
        design = design_step(design, momentum, passive, jnp.sum(jnp.abs(momentum)), jnp.sum(design), total_cells)
    return design, momentum, displacement
```

```python
import functools

import jax
import jax.numpy as jnp
from jax import lax
from jax.experimental import pallas as pl
from jax.experimental.pallas import tpu as pltpu
from jax.sharding import PartitionSpec as P

SWEEPS = 5
DESIGN_ITERS = 2
HALO = 7
WIDE = HALO - 1
XS, YLS, CORES = 4, 2, 2

stiff_floor = 0.01
mass_shift = 0.1
spectrum_low = 0.05
spectrum_high = 2.0
moment_decay = 0.8
step_size = 0.1
volume_pull = 0.5
volume_target = 0.4
density_floor = 0.001

F32 = jnp.float32


def chebyshev_factors():
    centre = 0.5 * (spectrum_high + spectrum_low)
    half_width = 0.5 * (spectrum_high - spectrum_low)
    ratio_one = centre / half_width
    previous = 1.0 / ratio_one
    factors = []
    for _ in range(SWEEPS - 1):
        current = 1.0 / (2.0 * ratio_one - previous)
        factors.append((current * previous, 2.0 * current / half_width))
        previous = current
    return 1.0 / centre, factors


def passive_apply(design, passive):
    return jnp.where(passive == 1, density_floor, jnp.where(passive == 2, 1.0, design))


def kernel(
    dims,
    density_ref, passive_ref, support_ref, nodes_ref, force_ref, weight_ref, body_ref,
    new_ref, moment_ref, disp_ref,
    design, support, passive, source, stiff, coef, gain, direct, resid, sens, moved_x,
    part, pair_in, pair_out, row_in, filt, msg, slots_one, slots_two,
    load_sems, body_send, body_recv, sup_send, sup_recv, supf_send, supf_recv,
    des_send, des_recv, desf_send, desf_recv,
    pair_send, pair_recv, row_send, row_recv, gath_send, gath_recv, gatf_send, gatf_recv,
    one_send, one_recv, two_send, two_recv, disp_sem,
):
    loads, bricks, cells_x, size_y, size_z, nodes = dims
    rows_hi = loads // CORES
    zs = bricks // (XS * YLS)
    slab = size_y // loads
    half = size_y // CORES
    ext = cells_x + 2 * HALO
    total_x = bricks * cells_x
    total_cells = float(total_x * size_y * size_z)
    last = HALO + cells_x
    local_loads = body_ref.shape[0]

    load = lax.axis_index("load")
    brick = lax.axis_index("brick")
    core = lax.rem(load, CORES)
    row = load // CORES
    at_x = lax.rem(brick, XS)
    at_yl = lax.rem(brick // XS, YLS)
    at_z = brick // (XS * YLS)
    has_low = brick > 0
    has_high = brick < bricks - 1
    partner = {"load": row * CORES + 1 - core, "brick": brick}

    def device(load_index, brick_index):
        return {"load": load_index, "brick": brick_index}

    group_one = rows_hi * YLS * CORES
    me_one = (row * YLS + at_yl) * CORES + core
    group_two = zs * XS
    me_two = at_z * XS + at_x

    def member_one(index):
        other_core = lax.rem(index, CORES)
        other_yl = lax.rem(index // CORES, YLS)
        other_row = index // (CORES * YLS)
        return device(other_row * CORES + other_core, (at_z * YLS + other_yl) * XS + at_x)

    def member_two(index):
        return device(load, (index // XS * YLS + at_yl) * XS + lax.rem(index, XS))

    def remote(src, dst, send, recv, target):
        return pltpu.make_async_remote_copy(
            src_ref=src, dst_ref=dst, send_sem=send, recv_sem=recv,
            device_id=target, device_id_type=pl.DeviceIdType.MESH,
        )

    own = pl.ds(HALO, cells_x)
    loads_in = [
        pltpu.make_async_copy(density_ref, design.at[0, own], load_sems.at[0]),
        pltpu.make_async_copy(passive_ref, passive, load_sems.at[1]),
        pltpu.make_async_copy(support_ref, support.at[own], load_sems.at[2]),
        pltpu.make_async_copy(body_ref, source.at[:, own], load_sems.at[3]),
    ]
    for copy in loads_in:
        copy.start()

    barrier = pltpu.get_barrier_semaphore()

    def greet_one(k, carry):
        pl.semaphore_signal(barrier, 1, device_id=member_one(lax.rem(me_one + k, group_one)),
                            device_id_type=pl.DeviceIdType.MESH)
        return carry

    def greet_two(k, carry):
        pl.semaphore_signal(barrier, 1, device_id=member_two(lax.rem(me_two + k, group_two)),
                            device_id_type=pl.DeviceIdType.MESH)
        return carry

    @pl.when(has_low)
    def _():
        pl.semaphore_signal(barrier, 1, device_id=device(load, brick - 1),
                            device_id_type=pl.DeviceIdType.MESH)

    @pl.when(has_high)
    def _():
        pl.semaphore_signal(barrier, 1, device_id=device(load, brick + 1),
                            device_id_type=pl.DeviceIdType.MESH)

    lax.fori_loop(1, group_two, greet_two, 0)
    lax.fori_loop(1, group_one, greet_one, 0)
    sides = jnp.where(has_low, 1, 0) + jnp.where(has_high, 1, 0)
    pl.semaphore_wait(barrier, group_one + group_two - 2 + sides)

    low, high = device(load, brick - 1), device(load, brick + 1)
    mine = pl.ds(pl.multiple_of(core * half, half), half)
    others = pl.ds(pl.multiple_of((1 - core) * half, half), half)

    def halo_copies(src, src_first, dst, width, send, recv, lead, rows):
        cut = (lambda ref, first: ref.at[lead + (pl.ds(first, width),) + rows])
        down = remote(cut(src, src_first), cut(dst, last), send.at[0], recv.at[1], low)
        up = remote(cut(src, src_first + cells_x - width), cut(dst, HALO - width),
                    send.at[1], recv.at[0], high)
        return down, up

    def start_halo(copies):
        down, up = copies

        @pl.when(has_low)
        def _():
            down.start()

        @pl.when(has_high)
        def _():
            up.start()

    def landed(dst, width, recv, send, lead, rows, side):
        first = HALO - width if side == 0 else last
        ref = dst.at[lead + (pl.ds(first, width),) + rows]
        return remote(ref, ref, send.at[side], recv.at[side], partner)

    body_rows = (slice(None), slice(None))
    body_copies = halo_copies(body_ref, 0, source, WIDE, body_send, body_recv, (slice(None),), body_rows)
    start_halo(body_copies)
    sup_copies = halo_copies(support_ref, 0, support, WIDE, sup_send, sup_recv, (), (mine, slice(None)))
    start_halo(sup_copies)

    loads_in[0].wait()
    loads_in[1].wait()

    def first_design(layer, carry):
        design[0, layer + HALO] = passive_apply(design[0, layer + HALO], passive[layer])
        return carry

    lax.fori_loop(0, cells_x, first_design, 0)

    def send_design(step):
        copies = halo_copies(design, HALO, design, HALO, des_send.at[step], des_recv.at[step],
                             (step,), (mine, slice(None)))
        start_halo(copies)
        return copies

    def clear(first):
        zero = jnp.zeros((size_y, size_z), F32)
        for layer in range(first, first + HALO):
            for step in range(DESIGN_ITERS):
                design[step, layer] = zero
            support[layer] = jnp.ones((size_y, size_z), jnp.int32)
            for one in range(local_loads):
                source[one, layer] = zero

    @pl.when(jnp.logical_not(has_low))
    def _():
        clear(0)

    @pl.when(jnp.logical_not(has_high))
    def _():
        clear(last)

    design_copies = [send_design(0)]
    loads_in[2].wait()
    loads_in[3].wait()

    node = nodes_ref[...]
    node_row = lax.shift_right_logical(node, size_z.bit_length() - 1)
    node_col = lax.bitwise_and(node, size_z - 1)
    flat_rows = jnp.concatenate([node_row[i:i + 1] for i in range(local_loads)], axis=1)
    flat_cols = jnp.concatenate([node_col[i:i + 1] for i in range(local_loads)], axis=1)
    flat_force = jnp.concatenate([force_ref[i:i + 1] for i in range(local_loads)], axis=1)
    width = local_loads * nodes
    col_of = jnp.transpose(jnp.broadcast_to(flat_cols.astype(F32), (size_z, width)))
    force_of = jnp.transpose(jnp.broadcast_to(flat_force, (size_z, width)))
    lanes = lax.broadcasted_iota(jnp.int32, (width, size_z), 1).astype(F32)
    owner = lax.broadcasted_iota(jnp.int32, (width, size_z), 0) // nodes
    placed = jnp.where(lanes == col_of, force_of, 0.0)
    spread = jnp.concatenate(
        [jnp.where(owner == i, placed, 0.0) for i in range(local_loads)], axis=1
    )
    row_iota = lax.broadcasted_iota(jnp.int32, (size_y, width), 0)

    def add_points(layer, carry):
        base = (brick * cells_x + layer - HALO) * size_y
        hot = jnp.where(row_iota + base == flat_rows, 1.0, 0.0)
        found = jnp.dot(hot, spread, preferred_element_type=F32, precision=lax.Precision.HIGHEST)
        for one in range(local_loads):
            source[one, layer] = source[one, layer] + found[:, one * size_z:(one + 1) * size_z]
        return carry

    iota_y = lax.broadcasted_iota(jnp.int32, (size_y, size_z), 0)
    iota_z = lax.broadcasted_iota(jnp.int32, (size_y, size_z), 1)
    y_first, y_last = iota_y == 0, iota_y == size_y - 1
    z_first, z_last = iota_z == 0, iota_z == size_z - 1

    def y_up(value):
        return pltpu.roll(value, size_y - 1, 0)

    def y_down(value):
        return pltpu.roll(value, 1, 0)

    def z_up(value):
        return pltpu.roll(value, size_z - 1, 1)

    def z_down(value):
        return pltpu.roll(value, 1, 1)

    def inner_sides(value):
        return (
            jnp.where(y_last, 0.0, y_up(value)),
            jnp.where(y_first, 0.0, y_down(value)),
            jnp.where(z_last, 0.0, z_up(value)),
            jnp.where(z_first, 0.0, z_down(value)),
        )

    first_scale, factors = chebyshev_factors()

    def run(first, stop, body):
        lax.fori_loop(first + HALO, stop + HALO, lambda e, c: (body(e), c)[1], 0)

    def make_stiff(step):
        def body(e):
            at = brick * cells_x + e - HALO
            inside = jnp.where(jnp.logical_and(at >= 0, at < total_x), 1.0, 0.0).astype(F32)
            value = design[step, e]
            stiff[e] = inside * (stiff_floor + (1.0 - stiff_floor) * (value * value * value))
        return body

    def make_coef(step):
        def body(e):
            s = stiff[e]
            free = (1 - support[e]).astype(F32)
            sides = (stiff[e + 1], stiff[e - 1]) + inner_sides(s)
            faces = [0.5 * (s + side) for side in sides]
            total = faces[0]
            for face in faces[1:]:
                total = total + face
            scale = free / (free * (total + mass_shift * s) + (1.0 - free))
            outer = (None, None, y_last, y_first, z_last, z_first)
            for j in range(6):
                value = scale * faces[j]
                coef[j, e] = value if outer[j] is None else jnp.where(outer[j], 0.0, value)
            here = design[step, e]
            for one in range(local_loads):
                start = scale * (source[one, e] + weight_ref[one] * here)
                resid[one, e] = start
                direct[one, 0, e] = first_scale * start
        return body

    def make_sweep(k):
        keep, pull = factors[k]

        def body(e):
            c = [coef[j, e] for j in range(6)]
            for one in range(local_loads):
                d = direct[one, k, e]
                total = c[0] * direct[one, k, e + 1] + c[1] * direct[one, k, e - 1]
                total = total + (c[2] * y_up(d) + c[3] * y_down(d))
                total = total + (c[4] * z_up(d) + c[5] * z_down(d))
                left = (resid[one, e] - d) + total
                if k < SWEEPS - 2:
                    resid[one, e] = left
                    direct[one, k + 1, e] = keep * d + pull * left
                else:
                    full = keep * d + pull * left + d
                    for older in range(k):
                        full = full + direct[one, older, e]
                    moved_x[one, e] = full
        return body

    def make_sens(step):
        def body(e):
            total = None
            for one in range(local_loads):
                f = moved_x[one, e]
                gaps = None
                for beside in (moved_x[one, e + 1], moved_x[one, e - 1]) + inner_sides(f):
                    gap = f - beside
                    gaps = gap * gap if gaps is None else gaps + gap * gap
                value = mass_shift * (f * f) + 0.25 * gaps
                total = value if total is None else total + value
            here = design[step, e]
            sens[e] = (-3.0 * (1.0 - stiff_floor)) * (here * here) * total
        return body

    edge_count = (
        y_first.astype(F32) + y_last.astype(F32) + z_first.astype(F32) + z_last.astype(F32)
    )

    def filter_layer(e):
        at = brick * cells_x + e - HALO
        end = jnp.where(jnp.logical_or(at == 0, at == total_x - 1), 1.0, 0.0).astype(F32)
        value = sens[e]
        total = 2.0 * value + sens[e + 1] + sens[e - 1]
        for beside in inner_sides(value):
            total = total + beside
        part[e - HALO] = total / (8.0 - (edge_count + end))

    def slab_rows(index):
        return pl.ds(pl.multiple_of(index * slab, slab), slab)

    def other_row(k):
        return lax.rem(row + k, rows_hi)

    my_slab = slab_rows(load)

    for step in range(DESIGN_ITERS):
        final = step == DESIGN_ITERS - 1
        run(0, cells_x, make_stiff(step))
        if step == 0:
            run(0, cells_x, lambda e: add_points(e, 0))
        run(1, cells_x - 1, make_coef(step))
        for k in range(SWEEPS - 1):
            run(2 + k, cells_x - 2 - k, make_sweep(k))

        for side, there in ((0, has_low), (1, has_high)):
            first = HALO - WIDE if side == 0 else last

            @pl.when(there)
            def _(side=side, there=there, first=first, step=step):
                if step == 0:
                    landed(support, WIDE, sup_recv, sup_send, (), (mine, slice(None)), side).wait_recv()
                    ref = support.at[pl.ds(first, WIDE), mine]
                    remote(ref, ref, supf_send.at[side], supf_recv.at[side], partner).start()
                landed(design, HALO, des_recv.at[step], des_send.at[step], (step,), (mine, slice(None)), side).wait_recv()
                ref = design.at[step, pl.ds(0 if side == 0 else last, HALO), mine]
                remote(ref, ref, desf_send.at[step, side], desf_recv.at[step, side], partner).start()
                if step == 0:
                    landed(source, WIDE, body_recv, body_send, (slice(None),), body_rows, side).wait_recv()
                    ref = support.at[pl.ds(first, WIDE), others]
                    remote(ref, ref, supf_send.at[side], supf_recv.at[side], partner).wait_recv()
                ref = design.at[step, pl.ds(0 if side == 0 else last, HALO), others]
                remote(ref, ref, desf_send.at[step, side], desf_recv.at[step, side], partner).wait_recv()

        for side in (0, 1):
            low_end = (lambda a, b: (a, b)) if side == 0 else (lambda a, b: (cells_x - b, cells_x - a))
            run(*low_end(-HALO, 0), make_stiff(step))
            if step == 0:
                run(*low_end(-WIDE, 0), lambda e: add_points(e, 0))
            run(*low_end(-WIDE, 1), make_coef(step))
        for side in (0, 1):
            low_end = (lambda a, b: (a, b)) if side == 0 else (lambda a, b: (cells_x - b, cells_x - a))
            for k in range(SWEEPS - 1):
                run(*low_end(k + 1 - WIDE, 2 + k), make_sweep(k))
        if final:
            out_copy = pltpu.make_async_copy(moved_x.at[:, own], disp_ref, disp_sem)
            out_copy.start()
        run(-1, cells_x + 1, make_sens(step))
        run(0, cells_x, filter_layer)

        to_pair = []
        for k in range(rows_hi):
            index = other_row(k)
            rows = slab_rows(index * CORES + 1 - core)
            copy = remote(part.at[:, rows], pair_in.at[step, index], pair_send.at[step, k],
                          pair_recv.at[step, index], partner)
            copy.start()
            to_pair.append(copy)
        to_row = []
        order = sorted(range(1, rows_hi), key=lambda k: -min(k, rows_hi - k)) + [0]
        for k in order:
            index = other_row(k)
            rows = slab_rows(index * CORES + core)
            remote(part.at[:, rows], pair_in.at[step, index], pair_send.at[step, k],
                   pair_recv.at[step, index], partner).wait_recv()
            pair_out[step, k] = part[:, rows] + pair_in[step, index]
            if k:
                copy = remote(pair_out.at[step, k], row_in.at[step, k], row_send.at[step, k],
                              row_recv.at[step, k], device(index * CORES + core, brick))
                copy.start()
                to_row.append(copy)
        total = pair_out[step, 0]
        for copy, k in zip(to_row, order):
            copy.wait_recv()
            total = total + row_in[step, k]
        if final:
            total = moment_decay * filt[:, my_slab] + total
            moment_ref[...] = total
        else:
            filt[:, my_slab] = total

        here = design[step, own, my_slab]
        msg[step, 0] = jnp.concatenate(
            [jnp.sum(jnp.abs(total), axis=0), jnp.sum(here, axis=0)], axis=0)
        slots_one[step, me_one] = msg[step, 0]

        def copy_one(k):
            index = lax.rem(me_one + k, group_one)
            return remote(msg.at[step, 0], slots_one.at[step, me_one], one_send.at[step, k],
                          one_recv.at[step, me_one], member_one(index))

        def came_one(k):
            index = lax.rem(me_one + k, group_one)
            return remote(msg.at[step, 0], slots_one.at[step, index], one_send.at[step, k],
                          one_recv.at[step, index], member_one(index))

        def copy_two(k):
            index = lax.rem(me_two + k, group_two)
            return remote(msg.at[step, 1], slots_two.at[step, me_two], two_send.at[step, k],
                          two_recv.at[step, me_two], member_two(index))

        def came_two(k):
            index = lax.rem(me_two + k, group_two)
            return remote(msg.at[step, 1], slots_two.at[step, index], two_send.at[step, k],
                          two_recv.at[step, index], member_two(index))

        def each(count, action):
            lax.fori_loop(1, count, lambda k, c: (action(k), c)[1], 0)

        each(group_one, lambda k: copy_one(k).start())

        gathers = []
        if not final:
            for k in order[:-1]:
                index = other_row(k)
                copy = remote(filt.at[:, my_slab], filt.at[:, my_slab], gath_send.at[k],
                              gath_recv.at[k], device(index * CORES + core, brick))
                copy.start()
                gathers.append(copy)
            copy = remote(filt.at[:, my_slab], filt.at[:, my_slab], gatf_send.at[0],
                          gatf_recv.at[0], partner)
            copy.start()
            gathers.append(copy)

        each(group_one, lambda k: came_one(k).wait_recv())
        msg[step, 1] = jnp.sum(slots_one[step], axis=0)
        slots_two[step, me_two] = msg[step, 1]
        each(group_two, lambda k: copy_two(k).start())

        if not final:
            for k in order[:-1][::-1]:
                index = lax.rem(row + rows_hi - k, rows_hi)
                ref = filt.at[:, slab_rows(index * CORES + core)]
                remote(ref, ref, gath_send.at[k], gath_recv.at[k], partner).wait_recv()
                copy = remote(ref, ref, gatf_send.at[k], gatf_recv.at[k], partner)
                copy.start()
                gathers.append(copy)
            for k in [0] + order[:-1][::-1]:
                index = lax.rem(row + rows_hi - k, rows_hi)
                ref = filt.at[:, slab_rows(index * CORES + 1 - core)]
                remote(ref, ref, gatf_send.at[k], gatf_recv.at[k], partner).wait_recv()

        each(group_two, lambda k: came_two(k).wait_recv())
        sums = jnp.sum(slots_two[step], axis=0)
        abs_total = jnp.sum(sums[0:slab], keepdims=True)
        density_total = jnp.sum(sums[slab:2 * slab], keepdims=True)
        rate = step_size / (abs_total / total_cells + 1e-06)
        pull_down = volume_pull * (density_total / total_cells - volume_target)

        def updated(old, moment, kind):
            value = old - rate * moment - pull_down
            return passive_apply(jnp.clip(value, density_floor, 1.0), kind)

        if final:
            def last_design(layer, carry):
                new_ref[layer] = updated(design[step, layer + HALO, my_slab],
                                         moment_ref[layer], passive[layer, my_slab])
                return carry

            lax.fori_loop(0, cells_x, last_design, 0)
        else:
            def next_design(layer, carry):
                design[step + 1, layer + HALO] = updated(
                    design[step, layer + HALO], filt[layer], passive[layer])
                return carry

            lax.fori_loop(0, cells_x, next_design, 0)
            design_copies.append(send_design(step + 1))

        for copy in to_pair + to_row + gathers:
            copy.wait_send()
        each(group_one, lambda k: copy_one(k).wait_send())
        each(group_two, lambda k: copy_two(k).wait_send())

    for side, there in ((0, has_low), (1, has_high)):
        @pl.when(there)
        def _(side=side):
            body_copies[side].wait_send()
            sup_copies[side].wait_send()
            first = HALO - WIDE if side == 0 else last
            ref = support.at[pl.ds(first, WIDE), mine]
            remote(ref, ref, supf_send.at[side], supf_recv.at[side], partner).wait_send()
            for step in range(DESIGN_ITERS):
                design_copies[step][side].wait_send()
                ref = design.at[step, pl.ds(0 if side == 0 else last, HALO), mine]
                remote(ref, ref, desf_send.at[step, side], desf_recv.at[step, side], partner).wait_send()
    out_copy.wait()


def body(dims, density, passive, support, load_nodes, load_force, self_weight, body_force):
    loads, bricks, cells_x, size_y, size_z, nodes = dims
    local_loads = body_force.shape[0]
    rows_hi = loads // CORES
    zs = bricks // (XS * YLS)
    slab = size_y // loads
    ext = cells_x + 2 * HALO
    group_one, group_two = loads * YLS, zs * XS
    steps = DESIGN_ITERS
    layer = (size_y, size_z)
    vmem = pltpu.VMEM
    dma = pltpu.SemaphoreType.DMA
    space_any = pl.BlockSpec(memory_space=pl.ANY)
    space_vmem = pl.BlockSpec(memory_space=pltpu.VMEM)
    space_smem = pl.BlockSpec(memory_space=pltpu.SMEM)
    piece = (cells_x, slab, size_z)
    return pl.pallas_call(
        functools.partial(kernel, dims),
        out_shape=(
            jax.ShapeDtypeStruct((cells_x, slab, size_z), F32),
            jax.ShapeDtypeStruct((cells_x, slab, size_z), F32),
            jax.ShapeDtypeStruct((local_loads, cells_x) + layer, F32),
        ),
        in_specs=[space_any, space_any, space_any, space_vmem, space_vmem, space_smem, space_any],
        out_specs=(space_vmem, space_vmem, space_any),
        scratch_shapes=[
            vmem((steps, ext) + layer, F32),
            vmem((ext,) + layer, jnp.int32),
            vmem((cells_x,) + layer, jnp.int32),
            vmem((local_loads, ext) + layer, F32),
            vmem((ext,) + layer, F32),
            vmem((6, ext) + layer, F32),
            vmem((1,) + layer, F32),
            vmem((local_loads, SWEEPS - 1, ext) + layer, F32),
            vmem((local_loads, ext) + layer, F32),
            vmem((ext,) + layer, F32),
            vmem((local_loads, ext) + layer, F32),
            vmem((cells_x,) + layer, F32),
            vmem((steps, rows_hi) + piece, F32),
            vmem((steps, rows_hi) + piece, F32),
            vmem((steps, rows_hi) + piece, F32),
            vmem((cells_x,) + layer, F32),
            vmem((steps, 2, 2 * slab, size_z), F32),
            vmem((steps, group_one, 2 * slab, size_z), F32),
            vmem((steps, group_two, 2 * slab, size_z), F32),
            dma((4,)),
            dma((2,)), dma((2,)),
            dma((2,)), dma((2,)), dma((2,)), dma((2,)),
            dma((steps, 2)), dma((steps, 2)), dma((steps, 2)), dma((steps, 2)),
            dma((steps, rows_hi)), dma((steps, rows_hi)),
            dma((steps, rows_hi)), dma((steps, rows_hi)),
            dma((rows_hi,)), dma((rows_hi,)), dma((rows_hi,)), dma((rows_hi,)),
            dma((steps, group_one)), dma((steps, group_one)),
            dma((steps, group_two)), dma((steps, group_two)),
            dma,
        ],
        compiler_params=pltpu.CompilerParams(collective_id=0, has_side_effects=True),
    )(density, passive, support, load_nodes, load_force, self_weight, body_force)


def solution(mesh):
    placed = (
        P("brick", None, None),
        P("brick", None, None),
        P("brick", None, None),
        P("load", None),
        P("load", None),
        P("load"),
        P("load", "brick", None, None),
    )

    def whole(*args):
        loads, bricks = mesh.shape["load"], mesh.shape["brick"]
        cells, size_y, size_z = args[0].shape
        dims = (loads, bricks, cells // bricks, size_y, size_z, args[3].shape[1])
        return jax.shard_map(
            functools.partial(body, dims),
            mesh=mesh,
            in_specs=placed,
            out_specs=(
                P("brick", "load", None),
                P("brick", "load", None),
                P("load", "brick", None, None),
            ),
            check_vma=False,
        )(*args)

    return whole
```

```python
import functools

import jax
import jax.numpy as jnp
from jax import lax
from jax.experimental import pallas as pl
from jax.experimental.pallas import tpu as pltpu
from jax.sharding import PartitionSpec as P

SWEEPS = 5
DESIGN_ITERS = 2
HALO = 7
WIDE = HALO - 1
PIECES = 4
PAD = 8
XS, YLS, CORES = 4, 2, 2

stiff_floor = 0.01
mass_shift = 0.1
spectrum_low = 0.05
spectrum_high = 2.0
moment_decay = 0.8
step_size = 0.1
volume_pull = 0.5
volume_target = 0.4
density_floor = 0.001

F32 = jnp.float32


def chebyshev_factors():
    centre = 0.5 * (spectrum_high + spectrum_low)
    half_width = 0.5 * (spectrum_high - spectrum_low)
    ratio_one = centre / half_width
    previous = 1.0 / ratio_one
    factors = []
    for _ in range(SWEEPS - 1):
        current = 1.0 / (2.0 * ratio_one - previous)
        factors.append((current * previous, 2.0 * current / half_width))
        previous = current
    return 1.0 / centre, factors


def passive_apply(design, passive):
    return jnp.where(passive == 1, density_floor, jnp.where(passive == 2, 1.0, design))


def kernel(
    dims,
    density_ref, passive_ref, support_ref, nodes_ref, force_ref, weight_ref, body_ref,
    new_ref, moment_ref, disp_ref,
    design, support, passive, source, points, stiff, coef, direct, resid, sens, moved_x,
    part, pair_in, pair_out, row_in, filt, msg, slots_one, slots_two,
    load_sems, body_send, body_recv, sup_send, sup_recv, supf_send, supf_recv,
    des_send, des_recv, desf_send, desf_recv,
    pair_send, pair_recv, row_send, row_recv, gath_send, gath_recv, gatf_send, gatf_recv,
    one_send, one_recv, two_send, two_recv, disp_sem, hello, column_in, partner_in,
):
    loads, bricks, cells_x, size_y, size_z, nodes = dims
    rows_hi = loads // CORES
    zs = bricks // (XS * YLS)
    slab = size_y // loads
    half = size_y // CORES
    ext = cells_x + 2 * HALO
    total_x = bricks * cells_x
    total_cells = float(total_x * size_y * size_z)
    last = HALO + cells_x
    local_loads = body_ref.shape[0]

    load = lax.axis_index("load")
    brick = lax.axis_index("brick")
    core = lax.rem(load, CORES)
    row = load // CORES
    at_x = lax.rem(brick, XS)
    at_yl = lax.rem(brick // XS, YLS)
    at_z = brick // (XS * YLS)
    has_low = brick > 0
    has_high = brick < bricks - 1
    partner = {"load": row * CORES + 1 - core, "brick": brick}

    def device(load_index, brick_index):
        return {"load": load_index, "brick": brick_index}

    group_one = rows_hi * YLS * CORES
    me_one = (row * YLS + at_yl) * CORES + core
    group_two = zs * XS
    me_two = at_z * XS + at_x

    def member_one(index):
        other_core = lax.rem(index, CORES)
        other_yl = lax.rem(index // CORES, YLS)
        other_row = index // (CORES * YLS)
        return device(other_row * CORES + other_core, (at_z * YLS + other_yl) * XS + at_x)

    def member_two(index):
        return device(load, (index // XS * YLS + at_yl) * XS + lax.rem(index, XS))

    def remote(src, dst, send, recv, target):
        return pltpu.make_async_remote_copy(
            src_ref=src, dst_ref=dst, send_sem=send, recv_sem=recv,
            device_id=target, device_id_type=pl.DeviceIdType.MESH,
        )

    own = pl.ds(HALO, cells_x)
    loads_in = [
        pltpu.make_async_copy(density_ref, design.at[0, own], load_sems.at[0]),
        pltpu.make_async_copy(passive_ref, passive, load_sems.at[1]),
        pltpu.make_async_copy(support_ref, support.at[own], load_sems.at[2]),
        pltpu.make_async_copy(body_ref, source.at[:, own], load_sems.at[3]),
    ]
    for copy in loads_in:
        copy.start()

    barrier = pltpu.get_barrier_semaphore()
    size_ring = {"y": YLS * rows_hi, "z": zs}

    def ring_peer(axis, shift):
        count = size_ring[axis]
        if axis == "z":
            there = lax.rem(at_z + shift + count, count)
            return device(load, (there * YLS + at_yl) * XS + at_x)
        there = lax.rem(row * YLS + at_yl + shift + count, count)
        return device(there // YLS * CORES + core, (at_z * YLS + lax.rem(there, YLS)) * XS + at_x)

    def x_peer(shift):
        return device(load, (at_z * YLS + at_yl) * XS + lax.rem(at_x + shift, XS))

    def signal(semaphore, target):
        pl.semaphore_signal(semaphore, 1, device_id=target, device_id_type=pl.DeviceIdType.MESH)

    @pl.when(has_low)
    def _():
        signal(barrier, device(load, brick - 1))

    @pl.when(has_high)
    def _():
        signal(barrier, device(load, brick + 1))

    signal(barrier, partner)
    for shift in range(1, XS):
        signal(barrier, x_peer(shift))
    for axis in ("y", "z"):
        for shift in (1, -1):
            signal(barrier, ring_peer(axis, shift))
    sides = jnp.where(has_low, 1, 0) + jnp.where(has_high, 1, 0)
    pl.semaphore_wait(barrier, 1 + (XS - 1) + 4 + sides)

    def pass_on(wave):
        for i, axis in enumerate(("y", "z")):
            waves = size_ring[axis] // 2 - 1
            for j, shift in enumerate((1, -1)):
                if 0 < wave <= waves:
                    pl.semaphore_wait(hello.at[i, j, wave - 1], 1)
                if wave < waves:
                    signal(hello.at[i, j, wave], ring_peer(axis, -shift))

    def rings_known():
        for shift in range(1, XS):
            signal(column_in, x_peer(shift))
        signal(partner_in, partner)

    low, high = device(load, brick - 1), device(load, brick + 1)
    mine = pl.ds(pl.multiple_of(core * half, half), half)
    others = pl.ds(pl.multiple_of((1 - core) * half, half), half)

    def halo_copies(src, src_first, dst, width, send, recv, lead, rows):
        cut = (lambda ref, first: ref.at[lead + (pl.ds(first, width),) + rows])
        down = remote(cut(src, src_first), cut(dst, last), send.at[0], recv.at[1], low)
        up = remote(cut(src, src_first + cells_x - width), cut(dst, HALO - width),
                    send.at[1], recv.at[0], high)
        return down, up

    def start_halo(copies):
        down, up = copies

        @pl.when(has_low)
        def _():
            down.start()

        @pl.when(has_high)
        def _():
            up.start()

    def landed(dst, width, recv, send, lead, rows, side):
        first = HALO - width if side == 0 else last
        ref = dst.at[lead + (pl.ds(first, width),) + rows]
        return remote(ref, ref, send.at[side], recv.at[side], partner)

    body_rows = (slice(None), slice(None))
    body_copies = halo_copies(body_ref, 0, source, WIDE, body_send, body_recv, (slice(None),), body_rows)
    sup_copies = halo_copies(support_ref, 0, support, WIDE, sup_send, sup_recv, (), (mine, slice(None)))
    start_halo(sup_copies)

    loads_in[0].wait()
    loads_in[1].wait()

    def first_design(layer, carry):
        design[0, layer + HALO] = passive_apply(design[0, layer + HALO], passive[layer])
        return carry

    lax.fori_loop(0, cells_x, first_design, 0)

    def send_design(step):
        copies = halo_copies(design, HALO, design, HALO, des_send.at[step], des_recv.at[step],
                             (step,), (mine, slice(None)))
        start_halo(copies)
        return copies

    def clear(first):
        zero = jnp.zeros((size_y, size_z), F32)
        for layer in range(first, first + HALO):
            for step in range(DESIGN_ITERS):
                design[step, layer] = zero
            support[layer] = jnp.ones((size_y, size_z), jnp.int32)
            for one in range(local_loads):
                source[one, layer] = zero

    @pl.when(jnp.logical_not(has_low))
    def _():
        clear(0)

    @pl.when(jnp.logical_not(has_high))
    def _():
        clear(last)

    design_copies = [send_design(0)]
    start_halo(body_copies)
    pass_on(0)

    blank = jnp.zeros((PAD, size_z), F32)

    def clear_pads(layer, carry):
        for edge in (pl.ds(0, PAD), pl.ds(PAD + size_y, PAD)):
            stiff[layer, edge] = blank
            sens[layer, edge] = blank
            for one in range(local_loads):
                moved_x[one, layer, edge] = blank
                for k in range(SWEEPS - 1):
                    direct[one][k][layer, edge] = blank
        return carry

    lax.fori_loop(0, ext, clear_pads, 0)
    pass_on(1)
    loads_in[2].wait()
    loads_in[3].wait()

    node = nodes_ref[...]
    node_row = lax.shift_right_logical(node, size_z.bit_length() - 1)
    node_col = lax.bitwise_and(node, size_z - 1)
    flat_rows = jnp.concatenate([node_row[i:i + 1] for i in range(local_loads)], axis=1)
    flat_cols = jnp.concatenate([node_col[i:i + 1] for i in range(local_loads)], axis=1)
    flat_force = jnp.concatenate([force_ref[i:i + 1] for i in range(local_loads)], axis=1)
    width = local_loads * nodes
    col_of = jnp.transpose(jnp.broadcast_to(flat_cols.astype(F32), (size_z, width)))
    force_of = jnp.transpose(jnp.broadcast_to(flat_force, (size_z, width)))
    lanes = lax.broadcasted_iota(jnp.int32, (width, size_z), 1).astype(F32)
    owner = lax.broadcasted_iota(jnp.int32, (width, size_z), 0) // nodes
    placed = jnp.where(lanes == col_of, force_of, 0.0)
    spread = jnp.concatenate(
        [jnp.where(owner == i, placed, 0.0) for i in range(local_loads)], axis=1
    )
    batch = 4
    row_iota = lax.broadcasted_iota(jnp.int32, (batch * size_y, width), 0)

    def find_points(turn, carry):
        layer = turn * batch + HALO - WIDE
        base = (brick * cells_x + layer - HALO) * size_y
        hot = jnp.where(row_iota + base == flat_rows, 1.0, 0.0)
        found = jnp.dot(hot, spread, preferred_element_type=F32, precision=lax.Precision.HIGHEST)
        for i in range(batch):
            for one in range(local_loads):
                points[one, layer + i] = found[
                    i * size_y:(i + 1) * size_y, one * size_z:(one + 1) * size_z]
        return carry

    assert (cells_x + 2 * WIDE) % batch == 0
    lax.fori_loop(0, (cells_x + 2 * WIDE) // batch, find_points, 0)
    pass_on(2)

    iota_y = lax.broadcasted_iota(jnp.int32, (size_y, size_z), 0)
    iota_z = lax.broadcasted_iota(jnp.int32, (size_y, size_z), 1)
    y_first, y_last = iota_y == 0, iota_y == size_y - 1
    z_first, z_last = iota_z == 0, iota_z == size_z - 1
    piece_rows = size_y // PIECES
    rows_in = pl.ds(PAD, size_y)
    rows_next = pl.ds(PAD + 1, size_y)
    rows_back = pl.ds(PAD - 1, size_y)

    def z_up(value):
        return pltpu.roll(value, size_z - 1, 1)

    def z_down(value):
        return pltpu.roll(value, 1, 1)

    def z_sides(value):
        return jnp.where(z_last, 0.0, z_up(value)), jnp.where(z_first, 0.0, z_down(value))

    first_scale, factors = chebyshev_factors()

    def run(first, stop, body, most=4):
        count = stop - first
        group = max(n for n in range(1, most + 1) if count % n == 0)

        def turn(index, carry):
            for i in range(group):
                body(first + HALO + index * group + i)
            return carry

        lax.fori_loop(0, count // group, turn, 0)

    def make_stiff(step):
        def body(e):
            at = brick * cells_x + e - HALO
            inside = jnp.where(jnp.logical_and(at >= 0, at < total_x), 1.0, 0.0).astype(F32)
            value = design[step, e]
            stiff[e, rows_in] = inside * (stiff_floor + (1.0 - stiff_floor) * (value * value * value))
        return body

    def make_coef(step):
        def body(e):
            s = stiff[e, rows_in]
            free = (1 - support[e]).astype(F32)
            sides = (stiff[e + 1, rows_in], stiff[e - 1, rows_in],
                     stiff[e, rows_next], stiff[e, rows_back]) + z_sides(s)
            faces = [0.5 * (s + side) for side in sides]
            total = faces[0]
            for face in faces[1:]:
                total = total + face
            scale = free / (free * (total + mass_shift * s) + (1.0 - free))
            outer = (None, None, None, None, z_last, z_first)
            for j in range(6):
                value = scale * faces[j]
                coef[j, e] = value if outer[j] is None else jnp.where(outer[j], 0.0, value)
            here = design[step, e]
            for one in range(local_loads):
                force = source[one, e]
                if step == 0:
                    force = force + points[one, e]
                    source[one, e] = force
                start = scale * (force + weight_ref[one] * here)
                resid[one, e] = start
                direct[one][0][e, rows_in] = first_scale * start
        return body

    def make_sweep(k):
        keep, pull = factors[k]

        def body(e):
            for part_rows in range(0, size_y, piece_rows):
                inner = pl.ds(part_rows, piece_rows)
                here, below, above = (pl.ds(PAD + part_rows + shift, piece_rows) for shift in (0, 1, -1))
                c = [coef[j, e, inner] for j in range(6)]
                for one in range(local_loads):
                    level = direct[one][k]
                    d = level[e, here]
                    total = c[0] * level[e + 1, here] + c[1] * level[e - 1, here]
                    total = total + (c[2] * level[e, below] + c[3] * level[e, above])
                    total = total + (c[4] * z_up(d) + c[5] * z_down(d))
                    left = (resid[one, e, inner] - d) + total
                    if k < SWEEPS - 2:
                        resid[one, e, inner] = left
                        direct[one][k + 1][e, here] = keep * d + pull * left
                    else:
                        full = keep * d + pull * left + d
                        for older in range(k):
                            full = full + direct[one][older][e, here]
                        moved_x[one, e, here] = full
        return body

    def make_sens(step):
        def body(e):
            total = squares = up_gaps = None
            for one in range(local_loads):
                f = moved_x[one, e, rows_in]
                square = f * f
                gaps = None
                for beside in (moved_x[one, e + 1, rows_in], moved_x[one, e - 1, rows_in],
                               moved_x[one, e, rows_next], moved_x[one, e, rows_back]):
                    gap = f - beside
                    gaps = gap * gap if gaps is None else gaps + gap * gap
                gap = f - jnp.where(z_last, 0.0, z_up(f))
                gap = gap * gap
                value = mass_shift * square + 0.25 * (gaps + gap)
                total = value if total is None else total + value
                squares = square if squares is None else squares + square
                up_gaps = gap if up_gaps is None else up_gaps + gap
            total = total + 0.25 * jnp.where(z_first, squares, z_down(up_gaps))
            here = design[step, e]
            sens[e, rows_in] = (-3.0 * (1.0 - stiff_floor)) * (here * here) * total
        return body

    edge_count = (
        y_first.astype(F32) + y_last.astype(F32) + z_first.astype(F32) + z_last.astype(F32)
    )

    def filter_layer(e):
        at = brick * cells_x + e - HALO
        end = jnp.where(jnp.logical_or(at == 0, at == total_x - 1), 1.0, 0.0).astype(F32)
        value = sens[e, rows_in]
        total = 2.0 * value + sens[e + 1, rows_in] + sens[e - 1, rows_in]
        total = total + sens[e, rows_next] + sens[e, rows_back]
        for beside in z_sides(value):
            total = total + beside
        part[e - HALO] = total / (8.0 - (edge_count + end))

    def slab_rows(index):
        return pl.ds(pl.multiple_of(index * slab, slab), slab)

    def other_row(k):
        return lax.rem(row + k, rows_hi)

    my_slab = slab_rows(load)

    for step in range(DESIGN_ITERS):
        final = step == DESIGN_ITERS - 1
        run(0, cells_x, make_stiff(step))
        run(1, cells_x - 1, make_coef(step), 5)
        if step == 0:
            pass_on(3)
            rings_known()
        for k in range(SWEEPS - 1):
            run(2 + k, cells_x - 2 - k, make_sweep(k))

        for side, there in ((0, has_low), (1, has_high)):
            first = HALO - WIDE if side == 0 else last

            @pl.when(there)
            def _(side=side, there=there, first=first, step=step):
                if step == 0:
                    landed(support, WIDE, sup_recv, sup_send, (), (mine, slice(None)), side).wait_recv()
                    ref = support.at[pl.ds(first, WIDE), mine]
                    remote(ref, ref, supf_send.at[side], supf_recv.at[side], partner).start()
                landed(design, HALO, des_recv.at[step], des_send.at[step], (step,), (mine, slice(None)), side).wait_recv()
                ref = design.at[step, pl.ds(0 if side == 0 else last, HALO), mine]
                remote(ref, ref, desf_send.at[step, side], desf_recv.at[step, side], partner).start()
                if step == 0:
                    landed(source, WIDE, body_recv, body_send, (slice(None),), body_rows, side).wait_recv()
                    ref = support.at[pl.ds(first, WIDE), others]
                    remote(ref, ref, supf_send.at[side], supf_recv.at[side], partner).wait_recv()
                ref = design.at[step, pl.ds(0 if side == 0 else last, HALO), others]
                remote(ref, ref, desf_send.at[step, side], desf_recv.at[step, side], partner).wait_recv()

        for side in (0, 1):
            low_end = (lambda a, b: (a, b)) if side == 0 else (lambda a, b: (cells_x - b, cells_x - a))
            run(*low_end(-HALO, 0), make_stiff(step))
            run(*low_end(-WIDE, 1), make_coef(step), 7)
        for side in (0, 1):
            low_end = (lambda a, b: (a, b)) if side == 0 else (lambda a, b: (cells_x - b, cells_x - a))
            for k in range(SWEEPS - 1):
                run(*low_end(k - WIDE, 2 + k), make_sweep(k))
        if final:
            out_copy = pltpu.make_async_copy(moved_x.at[:, own, rows_in], disp_ref, disp_sem)
            out_copy.start()
        run(-1, cells_x + 1, make_sens(step))
        run(0, cells_x, filter_layer)

        if step == 0:
            pl.semaphore_wait(column_in, XS - 1)
            pl.semaphore_wait(partner_in, 1)

        to_pair = []
        for k in range(rows_hi):
            index = other_row(k)
            rows = slab_rows(index * CORES + 1 - core)
            copy = remote(part.at[:, rows], pair_in.at[step, index], pair_send.at[step, k],
                          pair_recv.at[step, index], partner)
            copy.start()
            to_pair.append(copy)
        to_row = []
        order = sorted(range(1, rows_hi), key=lambda k: -min(k, rows_hi - k)) + [0]
        for k in order:
            index = other_row(k)
            rows = slab_rows(index * CORES + core)
            remote(part.at[:, rows], pair_in.at[step, index], pair_send.at[step, k],
                   pair_recv.at[step, index], partner).wait_recv()
            pair_out[step, k] = part[:, rows] + pair_in[step, index]
            if k:
                copy = remote(pair_out.at[step, k], row_in.at[step, k], row_send.at[step, k],
                              row_recv.at[step, k], device(index * CORES + core, brick))
                copy.start()
                to_row.append(copy)
        total = pair_out[step, 0]
        for copy, k in zip(to_row, order):
            copy.wait_recv()
            total = total + row_in[step, k]
        if final:
            total = moment_decay * filt[:, my_slab] + total
            moment_ref[...] = total
        else:
            filt[:, my_slab] = total

        here = design[step, own, my_slab]

        def fold(value):
            value = jnp.sum(jnp.sum(value, axis=0), axis=0, keepdims=True)
            return value + pltpu.roll(value, size_z // 2, 1)

        left_half = lax.broadcasted_iota(jnp.int32, (1, size_z), 1) < size_z // 2
        message = jnp.where(left_half, fold(jnp.abs(total)), fold(here))

        def share(message, stage, slots, send, recv, me, count, member):
            first_row = pl.ds(0, 1)
            msg[step, stage, first_row] = message
            slots[step, me, first_row] = message
            for k in range(1, count):
                remote(msg.at[step, stage, first_row], slots.at[step, me, first_row], send.at[step],
                       recv.at[step], member(lax.rem(me + k, count))).start()

            def finish():
                ref = slots.at[step, pl.ds(0, count - 1), first_row]
                remote(ref, ref, send.at[step], recv.at[step], partner).wait_recv()
                return jnp.sum(slots[step, :, first_row], axis=0)

            def drain():
                ref = slots.at[step, pl.ds(0, count - 1), first_row]
                remote(ref, ref, send.at[step], recv.at[step], partner).wait_send()

            return finish, drain

        finish_one, drain_one = share(message, 0, slots_one, one_send, one_recv, me_one, group_one, member_one)

        gathers = []
        if not final:
            for k in order[:-1]:
                index = other_row(k)
                copy = remote(filt.at[:, my_slab], filt.at[:, my_slab], gath_send.at[k],
                              gath_recv.at[k], device(index * CORES + core, brick))
                copy.start()
                gathers.append(copy)
            copy = remote(filt.at[:, my_slab], filt.at[:, my_slab], gatf_send.at[0],
                          gatf_recv.at[0], partner)
            copy.start()
            gathers.append(copy)

        finish_two, drain_two = share(finish_one(), 1, slots_two, two_send, two_recv, me_two, group_two, member_two)

        if not final:
            for k in order[:-1][::-1]:
                index = lax.rem(row + rows_hi - k, rows_hi)
                ref = filt.at[:, slab_rows(index * CORES + core)]
                remote(ref, ref, gath_send.at[k], gath_recv.at[k], partner).wait_recv()
                copy = remote(ref, ref, gatf_send.at[k], gatf_recv.at[k], partner)
                copy.start()
                gathers.append(copy)
            for k in [0] + order[:-1][::-1]:
                index = lax.rem(row + rows_hi - k, rows_hi)
                ref = filt.at[:, slab_rows(index * CORES + 1 - core)]
                remote(ref, ref, gatf_send.at[k], gatf_recv.at[k], partner).wait_recv()

        sums = finish_two()
        abs_total = jnp.sum(jnp.where(left_half, sums, 0.0), keepdims=True)
        density_total = jnp.sum(jnp.where(left_half, 0.0, sums), keepdims=True)
        rate = step_size / (abs_total / total_cells + 1e-06)
        pull_down = volume_pull * (density_total / total_cells - volume_target)

        def updated(old, moment, kind):
            value = old - rate * moment - pull_down
            return passive_apply(jnp.clip(value, density_floor, 1.0), kind)

        if final:
            def last_design(layer, carry):
                new_ref[layer] = updated(design[step, layer + HALO, my_slab],
                                         moment_ref[layer], passive[layer, my_slab])
                return carry

            lax.fori_loop(0, cells_x, last_design, 0)
        else:
            def next_design(layer, carry):
                design[step + 1, layer + HALO] = updated(
                    design[step, layer + HALO], filt[layer], passive[layer])
                return carry

            lax.fori_loop(0, cells_x, next_design, 0)
            design_copies.append(send_design(step + 1))

        for copy in to_pair + to_row + gathers:
            copy.wait_send()
        drain_one()
        drain_two()

    for side, there in ((0, has_low), (1, has_high)):
        @pl.when(there)
        def _(side=side):
            body_copies[side].wait_send()
            sup_copies[side].wait_send()
            first = HALO - WIDE if side == 0 else last
            ref = support.at[pl.ds(first, WIDE), mine]
            remote(ref, ref, supf_send.at[side], supf_recv.at[side], partner).wait_send()
            for step in range(DESIGN_ITERS):
                design_copies[step][side].wait_send()
                ref = design.at[step, pl.ds(0 if side == 0 else last, HALO), mine]
                remote(ref, ref, desf_send.at[step, side], desf_recv.at[step, side], partner).wait_send()
    out_copy.wait()


def body(dims, density, passive, support, load_nodes, load_force, self_weight, body_force):
    loads, bricks, cells_x, size_y, size_z, nodes = dims
    local_loads = body_force.shape[0]
    rows_hi = loads // CORES
    zs = bricks // (XS * YLS)
    slab = size_y // loads
    ext = cells_x + 2 * HALO
    group_one, group_two = loads * YLS, zs * XS
    steps = DESIGN_ITERS
    layer = (size_y, size_z)
    padded = (size_y + 2 * PAD, size_z)
    vmem = pltpu.VMEM
    dma, regular = pltpu.SemaphoreType.DMA, pltpu.SemaphoreType.REGULAR
    space_any = pl.BlockSpec(memory_space=pl.ANY)
    space_vmem = pl.BlockSpec(memory_space=pltpu.VMEM)
    space_smem = pl.BlockSpec(memory_space=pltpu.SMEM)
    piece = (cells_x, slab, size_z)
    results = pl.pallas_call(
        functools.partial(kernel, dims),
        out_shape=(
            jax.ShapeDtypeStruct((cells_x, slab, size_z), F32),
            jax.ShapeDtypeStruct((cells_x, slab, size_z), F32),
            jax.ShapeDtypeStruct((local_loads, cells_x) + layer, F32),
        ),
        in_specs=[space_any, space_any, space_any, space_vmem, space_vmem, space_smem, space_any],
        out_specs=(space_vmem, space_vmem, space_any),
        scratch_shapes=[
            vmem((steps, ext) + layer, F32),
            vmem((ext,) + layer, jnp.int32),
            vmem((cells_x,) + layer, jnp.int32),
            vmem((local_loads, ext) + layer, F32),
            vmem((local_loads, ext) + layer, F32),
            vmem((ext,) + padded, F32),
            vmem((6, ext) + layer, F32),
            ((vmem((ext,) + padded, F32),) * (SWEEPS - 1),) * local_loads,
            vmem((local_loads, ext) + layer, F32),
            vmem((ext,) + padded, F32),
            vmem((local_loads, ext) + padded, F32),
            vmem((cells_x,) + layer, F32),
            vmem((steps, rows_hi) + piece, F32),
            vmem((steps, rows_hi) + piece, F32),
            vmem((steps, rows_hi) + piece, F32),
            vmem((cells_x,) + layer, F32),
            vmem((steps, 2, 8, size_z), F32),
            vmem((steps, group_one, 8, size_z), F32),
            vmem((steps, group_two, 8, size_z), F32),
            dma((4,)),
            dma((2,)), dma((2,)),
            dma((2,)), dma((2,)), dma((2,)), dma((2,)),
            dma((steps, 2)), dma((steps, 2)), dma((steps, 2)), dma((steps, 2)),
            dma((steps, rows_hi)), dma((steps, rows_hi)),
            dma((steps, rows_hi)), dma((steps, rows_hi)),
            dma((rows_hi,)), dma((rows_hi,)), dma((rows_hi,)), dma((rows_hi,)),
            dma((steps,)), dma((steps,)), dma((steps,)), dma((steps,)),
            dma,
            regular((2, 2, max(YLS * rows_hi, zs) // 2)), regular, regular,
        ],
        compiler_params=pltpu.CompilerParams(collective_id=0, has_side_effects=True),
    )(density, passive, support, load_nodes, load_force, self_weight, body_force)
    parts = [(0, slice(0, cells_x)), (1, slice(0, cells_x))]
    parts += [(2, one) for one in range(local_loads)]
    return pl.pallas_call(
        functools.partial(hand_over, parts),
        out_shape=tuple(jax.ShapeDtypeStruct(value.shape, value.dtype) for value in results),
        in_specs=[space_any] * 3,
        out_specs=(space_any,) * 3,
        scratch_shapes=[vmem(value.shape, F32) for value in results]
        + [dma((len(parts),)), dma((len(parts),))],
    )(*results)


def hand_over(parts, *refs):
    sources, targets, held, (come, go) = refs[0:3], refs[3:6], refs[6:9], refs[9:]
    into = [pltpu.make_async_copy(sources[i].at[at], held[i].at[at], come.at[n]) for n, (i, at) in enumerate(parts)]
    out = [pltpu.make_async_copy(held[i].at[at], targets[i].at[at], go.at[n]) for n, (i, at) in enumerate(parts)]
    for copy in into:
        copy.start()
    for first, second in zip(into, out):
        first.wait()
        second.start()
    for copy in out:
        copy.wait()


def solution(mesh):
    placed = (
        P("brick", None, None),
        P("brick", None, None),
        P("brick", None, None),
        P("load", None),
        P("load", None),
        P("load"),
        P("load", "brick", None, None),
    )

    def whole(*args):
        loads, bricks = mesh.shape["load"], mesh.shape["brick"]
        cells, size_y, size_z = args[0].shape
        dims = (loads, bricks, cells // bricks, size_y, size_z, args[3].shape[1])
        return jax.shard_map(
            functools.partial(body, dims),
            mesh=mesh,
            in_specs=placed,
            out_specs=(
                P("brick", "load", None),
                P("brick", "load", None),
                P("load", "brick", None, None),
            ),
            check_vma=False,
        )(*args)

    return whole
```

```python
import functools

import jax
import jax.numpy as jnp
from jax import lax
from jax.experimental import pallas as pl
from jax.experimental.pallas import tpu as pltpu
from jax.sharding import PartitionSpec as P

SWEEPS = 5
DESIGN_ITERS = 2
HALO = 7
WIDE = HALO - 1
PIECES = 4
PAD = 8
XS, YLS, CORES = 4, 2, 2

stiff_floor = 0.01
mass_shift = 0.1
spectrum_low = 0.05
spectrum_high = 2.0
moment_decay = 0.8
step_size = 0.1
volume_pull = 0.5
volume_target = 0.4
density_floor = 0.001

F32 = jnp.float32


def chebyshev_factors():
    centre = 0.5 * (spectrum_high + spectrum_low)
    half_width = 0.5 * (spectrum_high - spectrum_low)
    ratio_one = centre / half_width
    previous = 1.0 / ratio_one
    factors = []
    for _ in range(SWEEPS - 1):
        current = 1.0 / (2.0 * ratio_one - previous)
        factors.append((current * previous, 2.0 * current / half_width))
        previous = current
    return 1.0 / centre, factors


def passive_apply(design, passive):
    return jnp.where(passive == 1, density_floor, jnp.where(passive == 2, 1.0, design))


def kernel(
    dims,
    density_ref, passive_ref, support_ref, nodes_ref, force_ref, weight_ref, body_ref,
    new_ref, moment_ref, disp_ref,
    design, support, passive, source, points, stiff, coef, direct, resid, sens, moved_x,
    part, pair_in, pair_out, row_in, filt, msg, slots_one, slots_two,
    load_sems, body_send, body_recv, sup_send, sup_recv, supf_send, supf_recv,
    des_send, des_recv, desf_send, desf_recv,
    pair_send, pair_recv, row_send, row_recv, gath_send, gath_recv, gatf_send, gatf_recv,
    pas_send, pas_recv, pasf_send, pasf_recv, fil_send, fil_recv, filf_send, filf_recv,
    one_send, one_recv, two_send, two_recv, disp_sem, hello, column_in, partner_in,
):
    loads, bricks, cells_x, size_y, size_z, nodes = dims
    rows_hi = loads // CORES
    zs = bricks // (XS * YLS)
    slab = size_y // loads
    half = size_y // CORES
    ext = cells_x + 2 * HALO
    total_x = bricks * cells_x
    total_cells = float(total_x * size_y * size_z)
    last = HALO + cells_x
    local_loads = body_ref.shape[0]

    load = lax.axis_index("load")
    brick = lax.axis_index("brick")
    core = lax.rem(load, CORES)
    row = load // CORES
    at_x = lax.rem(brick, XS)
    at_yl = lax.rem(brick // XS, YLS)
    at_z = brick // (XS * YLS)
    has_low = brick > 0
    has_high = brick < bricks - 1
    partner = {"load": row * CORES + 1 - core, "brick": brick}

    def device(load_index, brick_index):
        return {"load": load_index, "brick": brick_index}

    group_one = rows_hi * YLS * CORES
    me_one = (row * YLS + at_yl) * CORES + core
    group_two = zs * XS
    me_two = at_z * XS + at_x

    def member_one(index):
        other_core = lax.rem(index, CORES)
        other_yl = lax.rem(index // CORES, YLS)
        other_row = index // (CORES * YLS)
        return device(other_row * CORES + other_core, (at_z * YLS + other_yl) * XS + at_x)

    def member_two(index):
        return device(load, (index // XS * YLS + at_yl) * XS + lax.rem(index, XS))

    def remote(src, dst, send, recv, target):
        return pltpu.make_async_remote_copy(
            src_ref=src, dst_ref=dst, send_sem=send, recv_sem=recv,
            device_id=target, device_id_type=pl.DeviceIdType.MESH,
        )

    own = pl.ds(HALO, cells_x)
    loads_in = [
        pltpu.make_async_copy(density_ref, design.at[0, own], load_sems.at[0]),
        pltpu.make_async_copy(passive_ref, passive.at[own], load_sems.at[1]),
        pltpu.make_async_copy(support_ref, support.at[own], load_sems.at[2]),
        pltpu.make_async_copy(body_ref, source.at[:, own], load_sems.at[3]),
    ]
    for copy in loads_in:
        copy.start()

    barrier = pltpu.get_barrier_semaphore()
    size_ring = {"y": YLS * rows_hi, "z": zs}

    def ring_peer(axis, shift):
        count = size_ring[axis]
        if axis == "z":
            there = lax.rem(at_z + shift + count, count)
            return device(load, (there * YLS + at_yl) * XS + at_x)
        there = lax.rem(row * YLS + at_yl + shift + count, count)
        return device(there // YLS * CORES + core, (at_z * YLS + lax.rem(there, YLS)) * XS + at_x)

    def x_peer(shift):
        return device(load, (at_z * YLS + at_yl) * XS + lax.rem(at_x + shift, XS))

    def signal(semaphore, target):
        pl.semaphore_signal(semaphore, 1, device_id=target, device_id_type=pl.DeviceIdType.MESH)

    @pl.when(has_low)
    def _():
        signal(barrier, device(load, brick - 1))

    @pl.when(has_high)
    def _():
        signal(barrier, device(load, brick + 1))

    signal(barrier, partner)
    for shift in range(1, XS):
        signal(barrier, x_peer(shift))
    for axis in ("y", "z"):
        for shift in (1, -1):
            signal(barrier, ring_peer(axis, shift))
    sides = jnp.where(has_low, 1, 0) + jnp.where(has_high, 1, 0)
    pl.semaphore_wait(barrier, 1 + (XS - 1) + 4 + sides)

    def pass_on(wave):
        for i, axis in enumerate(("y", "z")):
            waves = size_ring[axis] // 2 - 1
            for j, shift in enumerate((1, -1)):
                if 0 < wave <= waves:
                    pl.semaphore_wait(hello.at[i, j, wave - 1], 1)
                if wave < waves:
                    signal(hello.at[i, j, wave], ring_peer(axis, -shift))

    def rings_known():
        for shift in range(1, XS):
            signal(column_in, x_peer(shift))
        signal(partner_in, partner)

    low, high = device(load, brick - 1), device(load, brick + 1)
    mine = pl.ds(pl.multiple_of(core * half, half), half)
    others = pl.ds(pl.multiple_of((1 - core) * half, half), half)

    def halo_copies(src, src_first, dst, width, send, recv, lead, rows):
        cut = (lambda ref, first: ref.at[lead + (pl.ds(first, width),) + rows])
        down = remote(cut(src, src_first), cut(dst, last), send.at[0], recv.at[1], low)
        up = remote(cut(src, src_first + cells_x - width), cut(dst, HALO - width),
                    send.at[1], recv.at[0], high)
        return down, up

    def start_halo(copies):
        down, up = copies

        @pl.when(has_low)
        def _():
            down.start()

        @pl.when(has_high)
        def _():
            up.start()

    def landed(dst, width, recv, send, lead, rows, side):
        first = HALO - width if side == 0 else last
        ref = dst.at[lead + (pl.ds(first, width),) + rows]
        return remote(ref, ref, send.at[side], recv.at[side], partner)

    body_rows = (slice(None), slice(None))
    body_copies = halo_copies(body_ref, 0, source, WIDE, body_send, body_recv, (slice(None),), body_rows)
    sup_copies = halo_copies(support_ref, 0, support, WIDE, sup_send, sup_recv, (), (mine, slice(None)))
    start_halo(sup_copies)

    loads_in[0].wait()
    loads_in[1].wait()

    def first_design(layer, carry):
        design[0, layer + HALO] = passive_apply(design[0, layer + HALO], passive[layer + HALO])
        return carry

    lax.fori_loop(0, cells_x, first_design, 0)

    def clear(first):
        zero = jnp.zeros((size_y, size_z), F32)
        for layer in range(first, first + HALO):
            for step in range(DESIGN_ITERS):
                design[step, layer] = zero
            support[layer] = jnp.ones((size_y, size_z), jnp.int32)
            for one in range(local_loads):
                source[one, layer] = zero

    @pl.when(jnp.logical_not(has_low))
    def _():
        clear(0)

    @pl.when(jnp.logical_not(has_high))
    def _():
        clear(last)

    half_rows = (mine, slice(None))
    des_copies = halo_copies(design, HALO, design, HALO, des_send, des_recv, (0,), half_rows)
    start_halo(des_copies)
    start_halo(body_copies)
    pas_copies = halo_copies(passive_ref, 0, passive, HALO, pas_send, pas_recv, (), half_rows)
    start_halo(pas_copies)
    pass_on(0)

    blank = jnp.zeros((PAD, size_z), F32)

    def clear_pads(layer, carry):
        for edge in (pl.ds(0, PAD), pl.ds(PAD + size_y, PAD)):
            stiff[layer, edge] = blank
            sens[layer, edge] = blank
            for one in range(local_loads):
                moved_x[one, layer, edge] = blank
                for k in range(SWEEPS - 1):
                    direct[one][k][layer, edge] = blank
        return carry

    lax.fori_loop(0, ext, clear_pads, 0)
    pass_on(1)
    loads_in[2].wait()
    loads_in[3].wait()

    node = nodes_ref[...]
    node_row = lax.shift_right_logical(node, size_z.bit_length() - 1)
    node_col = lax.bitwise_and(node, size_z - 1)
    flat_rows = jnp.concatenate([node_row[i:i + 1] for i in range(local_loads)], axis=1)
    flat_cols = jnp.concatenate([node_col[i:i + 1] for i in range(local_loads)], axis=1)
    flat_force = jnp.concatenate([force_ref[i:i + 1] for i in range(local_loads)], axis=1)
    width = local_loads * nodes
    col_of = jnp.transpose(jnp.broadcast_to(flat_cols.astype(F32), (size_z, width)))
    force_of = jnp.transpose(jnp.broadcast_to(flat_force, (size_z, width)))
    lanes = lax.broadcasted_iota(jnp.int32, (width, size_z), 1).astype(F32)
    owner = lax.broadcasted_iota(jnp.int32, (width, size_z), 0) // nodes
    placed = jnp.where(lanes == col_of, force_of, 0.0)
    spread = jnp.concatenate(
        [jnp.where(owner == i, placed, 0.0) for i in range(local_loads)], axis=1
    )
    batch = 4
    row_iota = lax.broadcasted_iota(jnp.int32, (batch * size_y, width), 0)

    def find_points(turn, carry):
        layer = turn * batch + HALO - WIDE
        base = (brick * cells_x + layer - HALO) * size_y
        hot = jnp.where(row_iota + base == flat_rows, 1.0, 0.0)
        found = jnp.dot(hot, spread, preferred_element_type=F32, precision=lax.Precision.HIGHEST)
        for i in range(batch):
            for one in range(local_loads):
                points[one, layer + i] = found[
                    i * size_y:(i + 1) * size_y, one * size_z:(one + 1) * size_z]
        return carry

    assert (cells_x + 2 * WIDE) % batch == 0
    lax.fori_loop(0, (cells_x + 2 * WIDE) // batch, find_points, 0)
    pass_on(2)

    iota_y = lax.broadcasted_iota(jnp.int32, (size_y, size_z), 0)
    iota_z = lax.broadcasted_iota(jnp.int32, (size_y, size_z), 1)
    y_first, y_last = iota_y == 0, iota_y == size_y - 1
    z_first, z_last = iota_z == 0, iota_z == size_z - 1
    piece_rows = size_y // PIECES
    rows_in = pl.ds(PAD, size_y)
    rows_next = pl.ds(PAD + 1, size_y)
    rows_back = pl.ds(PAD - 1, size_y)

    def z_up(value):
        return pltpu.roll(value, size_z - 1, 1)

    def z_down(value):
        return pltpu.roll(value, 1, 1)

    def z_sides(value):
        return jnp.where(z_last, 0.0, z_up(value)), jnp.where(z_first, 0.0, z_down(value))

    first_scale, factors = chebyshev_factors()

    def run(first, stop, body, most=4):
        count = stop - first
        group = max(n for n in range(1, most + 1) if count % n == 0)

        def turn(index, carry):
            for i in range(group):
                body(first + HALO + index * group + i)
            return carry

        lax.fori_loop(0, count // group, turn, 0)

    def make_stiff(step):
        def body(e):
            at = brick * cells_x + e - HALO
            inside = jnp.where(jnp.logical_and(at >= 0, at < total_x), 1.0, 0.0).astype(F32)
            value = design[step, e]
            stiff[e, rows_in] = inside * (stiff_floor + (1.0 - stiff_floor) * (value * value * value))
        return body

    def make_coef(step):
        def body(e):
            s = stiff[e, rows_in]
            free = (1 - support[e]).astype(F32)
            sides = (stiff[e + 1, rows_in], stiff[e - 1, rows_in],
                     stiff[e, rows_next], stiff[e, rows_back]) + z_sides(s)
            faces = [0.5 * (s + side) for side in sides]
            total = faces[0]
            for face in faces[1:]:
                total = total + face
            scale = free / (free * (total + mass_shift * s) + (1.0 - free))
            outer = (None, None, None, None, z_last, z_first)
            for j in range(6):
                value = scale * faces[j]
                coef[j, e] = value if outer[j] is None else jnp.where(outer[j], 0.0, value)
            here = design[step, e]
            for one in range(local_loads):
                force = source[one, e]
                if step == 0:
                    force = force + points[one, e]
                    source[one, e] = force
                start = scale * (force + weight_ref[one] * here)
                resid[one, e] = start
                direct[one][0][e, rows_in] = first_scale * start
        return body

    def make_sweep(k):
        keep, pull = factors[k]

        def body(e):
            for part_rows in range(0, size_y, piece_rows):
                inner = pl.ds(part_rows, piece_rows)
                here, below, above = (pl.ds(PAD + part_rows + shift, piece_rows) for shift in (0, 1, -1))
                c = [coef[j, e, inner] for j in range(6)]
                for one in range(local_loads):
                    level = direct[one][k]
                    d = level[e, here]
                    total = c[0] * level[e + 1, here] + c[1] * level[e - 1, here]
                    total = total + (c[2] * level[e, below] + c[3] * level[e, above])
                    total = total + (c[4] * z_up(d) + c[5] * z_down(d))
                    left = (resid[one, e, inner] - d) + total
                    if k < SWEEPS - 2:
                        resid[one, e, inner] = left
                        direct[one][k + 1][e, here] = keep * d + pull * left
                    else:
                        full = keep * d + pull * left + d
                        for older in range(k):
                            full = full + direct[one][older][e, here]
                        moved_x[one, e, here] = full
        return body

    def make_sens(step):
        def body(e):
            total = squares = up_gaps = None
            for one in range(local_loads):
                f = moved_x[one, e, rows_in]
                square = f * f
                gaps = None
                for beside in (moved_x[one, e + 1, rows_in], moved_x[one, e - 1, rows_in],
                               moved_x[one, e, rows_next], moved_x[one, e, rows_back]):
                    gap = f - beside
                    gaps = gap * gap if gaps is None else gaps + gap * gap
                gap = f - jnp.where(z_last, 0.0, z_up(f))
                gap = gap * gap
                value = mass_shift * square + 0.25 * (gaps + gap)
                total = value if total is None else total + value
                squares = square if squares is None else squares + square
                up_gaps = gap if up_gaps is None else up_gaps + gap
            total = total + 0.25 * jnp.where(z_first, squares, z_down(up_gaps))
            here = design[step, e]
            sens[e, rows_in] = (-3.0 * (1.0 - stiff_floor)) * (here * here) * total
        return body

    edge_count = (
        y_first.astype(F32) + y_last.astype(F32) + z_first.astype(F32) + z_last.astype(F32)
    )

    def filter_layer(e):
        at = brick * cells_x + e - HALO
        end = jnp.where(jnp.logical_or(at == 0, at == total_x - 1), 1.0, 0.0).astype(F32)
        value = sens[e, rows_in]
        total = 2.0 * value + sens[e + 1, rows_in] + sens[e - 1, rows_in]
        total = total + sens[e, rows_next] + sens[e, rows_back]
        for beside in z_sides(value):
            total = total + beside
        part[e - HALO] = total / (8.0 - (edge_count + end))

    def slab_rows(index):
        return pl.ds(pl.multiple_of(index * slab, slab), slab)

    def other_row(k):
        return lax.rem(row + k, rows_hi)

    my_slab = slab_rows(load)

    both_sides = ((0, has_low), (1, has_high))

    def to_partner(ref, lead, width, side, send, recv, rows):
        first = HALO - width if side == 0 else last
        ref = ref.at[lead + (pl.ds(first, width), rows)]
        return remote(ref, ref, send, recv, partner)

    def pass_to_partner(ref, lead, width, side, near, far):
        landed(ref, width, near[1], near[0], lead, half_rows, side).wait_recv()
        to_partner(ref, lead, width, side, far[0].at[side], far[1].at[side], mine).start()

    sup_sems, des_sems, pas_sems = (
        ((sup_send, sup_recv), (supf_send, supf_recv)),
        ((des_send, des_recv), (desf_send, desf_recv)),
        ((pas_send, pas_recv), (pasf_send, pasf_recv)),
    )
    halo_kinds = ((support, (), WIDE, sup_sems), (design, (0,), HALO, des_sems), (passive, (), HALO, pas_sems))

    def came_from_partner(kind, side):
        ref, lead, width, sems = kind
        to_partner(ref, lead, width, side, sems[1][0].at[side], sems[1][1].at[side], others).wait_recv()

    def pass_filtered(k):
        rows = slab_rows(lax.rem(row + rows_hi - k, rows_hi) * CORES + core)
        down = remote(filt.at[pl.ds(HALO, HALO), rows], filt.at[pl.ds(last, HALO), rows],
                      fil_send.at[k, 0], fil_recv.at[k, 1], low)
        up = remote(filt.at[pl.ds(cells_x, HALO), rows], filt.at[pl.ds(0, HALO), rows],
                    fil_send.at[k, 1], fil_recv.at[k, 0], high)
        return down, up

    def filtered_halo(k, side, whose):
        index = lax.rem(row + rows_hi - k, rows_hi) * CORES + whose
        return filt.at[pl.ds(0 if side == 0 else last, HALO), slab_rows(index)]

    for step in range(DESIGN_ITERS):
        final = step == DESIGN_ITERS - 1
        if step == 0:
            run(0, cells_x, make_stiff(step))
            run(1, cells_x - 1, make_coef(step), 5)
            pass_on(3)
            rings_known()
            for k in range(SWEEPS - 1):
                run(2 + k, cells_x - 2 - k, make_sweep(k))

            for side, there in both_sides:
                @pl.when(there)
                def _(side=side):
                    for ref, lead, width, (near, far) in halo_kinds[:2]:
                        pass_to_partner(ref, lead, width, side, near, far)

            for side, there in both_sides:
                @pl.when(there)
                def _(side=side):
                    landed(source, WIDE, body_recv, body_send, (slice(None),), body_rows, side).wait_recv()
                    for kind in halo_kinds[:2]:
                        came_from_partner(kind, side)

                low_end = (lambda a, b: (a, b)) if side == 0 else (lambda a, b: (cells_x - b, cells_x - a))
                run(*low_end(-HALO, 0), make_stiff(step))
                run(*low_end(-WIDE, 1), make_coef(step), 7)
                for k in range(SWEEPS - 1):
                    run(*low_end(k + 1 - WIDE, 2 + k), make_sweep(k), 7)

            for side, there in both_sides:
                @pl.when(there)
                def _(side=side):
                    ref, lead, width, (near, far) = halo_kinds[2]
                    pass_to_partner(ref, lead, width, side, near, far)
        else:
            run(-HALO, cells_x + HALO, make_stiff(step))
            run(-WIDE, cells_x + WIDE, make_coef(step))
            for k in range(SWEEPS - 1):
                run(k + 1 - WIDE, cells_x + WIDE - 1 - k, make_sweep(k), 5)
        if final:
            out_copy = pltpu.make_async_copy(moved_x.at[:, own, rows_in], disp_ref, disp_sem)
            out_copy.start()
        run(-1, cells_x + 1, make_sens(step))
        run(0, cells_x, filter_layer)

        if step == 0:
            pl.semaphore_wait(column_in, XS - 1)
            pl.semaphore_wait(partner_in, 1)

        to_pair = []
        for k in range(rows_hi):
            index = other_row(k)
            rows = slab_rows(index * CORES + 1 - core)
            copy = remote(part.at[:, rows], pair_in.at[step, index], pair_send.at[step, k],
                          pair_recv.at[step, index], partner)
            copy.start()
            to_pair.append(copy)
        to_row = []
        order = sorted(range(1, rows_hi), key=lambda k: -min(k, rows_hi - k)) + [0]
        for k in order:
            index = other_row(k)
            rows = slab_rows(index * CORES + core)
            remote(part.at[:, rows], pair_in.at[step, index], pair_send.at[step, k],
                   pair_recv.at[step, index], partner).wait_recv()
            pair_out[step, k] = part[:, rows] + pair_in[step, index]
            if k:
                copy = remote(pair_out.at[step, k], row_in.at[step, k], row_send.at[step, k],
                              row_recv.at[step, k], device(index * CORES + core, brick))
                copy.start()
                to_row.append(copy)
        total = pair_out[step, 0]
        for copy, k in zip(to_row, order):
            copy.wait_recv()
            total = total + row_in[step, k]
        if final:
            total = moment_decay * filt[own, my_slab] + total
            moment_ref[...] = total
        else:
            filt[own, my_slab] = total

        here = design[step, own, my_slab]

        def fold(value):
            value = jnp.sum(jnp.sum(value, axis=0), axis=0, keepdims=True)
            return value + pltpu.roll(value, size_z // 2, 1)

        left_half = lax.broadcasted_iota(jnp.int32, (1, size_z), 1) < size_z // 2
        message = jnp.where(left_half, fold(jnp.abs(total)), fold(here))

        def share(message, stage, slots, send, recv, me, count, member):
            first_row = pl.ds(0, 1)
            msg[step, stage, first_row] = message
            slots[step, me, first_row] = message
            for k in range(1, count):
                remote(msg.at[step, stage, first_row], slots.at[step, me, first_row], send.at[step],
                       recv.at[step], member(lax.rem(me + k, count))).start()

            def finish():
                ref = slots.at[step, pl.ds(0, count - 1), first_row]
                remote(ref, ref, send.at[step], recv.at[step], partner).wait_recv()
                return jnp.sum(slots[step, :, first_row], axis=0)

            def drain():
                ref = slots.at[step, pl.ds(0, count - 1), first_row]
                remote(ref, ref, send.at[step], recv.at[step], partner).wait_send()

            return finish, drain

        finish_one, drain_one = share(message, 0, slots_one, one_send, one_recv, me_one, group_one, member_one)

        gathers = []
        if not final:
            for k in order[:-1]:
                index = other_row(k)
                copy = remote(filt.at[own, my_slab], filt.at[own, my_slab], gath_send.at[k],
                              gath_recv.at[k], device(index * CORES + core, brick))
                copy.start()
                gathers.append(copy)
            start_halo(pass_filtered(0))
            copy = remote(filt.at[own, my_slab], filt.at[own, my_slab], gatf_send.at[0],
                          gatf_recv.at[0], partner)
            copy.start()
            gathers.append(copy)

        finish_two, drain_two = share(finish_one(), 1, slots_two, two_send, two_recv, me_two, group_two, member_two)

        if not final:
            for k in order[:-1][::-1]:
                index = lax.rem(row + rows_hi - k, rows_hi)
                ref = filt.at[own, slab_rows(index * CORES + core)]
                remote(ref, ref, gath_send.at[k], gath_recv.at[k], partner).wait_recv()
                start_halo(pass_filtered(k))
                copy = remote(ref, ref, gatf_send.at[k], gatf_recv.at[k], partner)
                copy.start()
                gathers.append(copy)
            came_in = [0] + order[:-1][::-1]
            for k in came_in:
                for side, there in both_sides:
                    @pl.when(there)
                    def _(k=k, side=side):
                        ref = filtered_halo(k, side, core)
                        remote(ref, ref, fil_send.at[k, side], fil_recv.at[k, side], partner).wait_recv()
                        remote(ref, ref, filf_send.at[k, side], filf_recv.at[k, side], partner).start()
            for k in came_in:
                index = lax.rem(row + rows_hi - k, rows_hi)
                ref = filt.at[own, slab_rows(index * CORES + 1 - core)]
                remote(ref, ref, gatf_send.at[k], gatf_recv.at[k], partner).wait_recv()
                for side, there in both_sides:
                    @pl.when(there)
                    def _(k=k, side=side):
                        ref = filtered_halo(k, side, 1 - core)
                        remote(ref, ref, filf_send.at[k, side], filf_recv.at[k, side], partner).wait_recv()
            for side, there in both_sides:
                @pl.when(there)
                def _(side=side):
                    came_from_partner(halo_kinds[2], side)

        sums = finish_two()
        abs_total = jnp.sum(jnp.where(left_half, sums, 0.0), keepdims=True)
        density_total = jnp.sum(jnp.where(left_half, 0.0, sums), keepdims=True)
        rate = step_size / (abs_total / total_cells + 1e-06)
        pull_down = volume_pull * (density_total / total_cells - volume_target)

        def updated(old, moment, kind):
            value = old - rate * moment - pull_down
            return passive_apply(jnp.clip(value, density_floor, 1.0), kind)

        if final:
            def last_design(layer, carry):
                new_ref[layer] = updated(design[step, layer + HALO, my_slab],
                                         moment_ref[layer], passive[layer + HALO, my_slab])
                return carry

            lax.fori_loop(0, cells_x, last_design, 0)
        else:
            def next_design(e):
                design[step + 1, e] = updated(design[step, e], filt[e], passive[e])

            @pl.when(has_low)
            def _():
                run(-HALO, 0, next_design, 7)

            run(0, cells_x, next_design, 6)

            @pl.when(has_high)
            def _():
                run(cells_x, cells_x + HALO, next_design, 7)

        for copy in to_pair + to_row + gathers:
            copy.wait_send()
        drain_one()
        drain_two()

    for side, there in both_sides:
        @pl.when(there)
        def _(side=side):
            for copies in (body_copies, sup_copies, des_copies, pas_copies):
                copies[side].wait_send()
            for ref, lead, width, sems in halo_kinds:
                to_partner(ref, lead, width, side, sems[1][0].at[side], sems[1][1].at[side], mine).wait_send()
            for k in range(rows_hi):
                pass_filtered(k)[side].wait_send()
                ref = filtered_halo(k, side, core)
                remote(ref, ref, filf_send.at[k, side], filf_recv.at[k, side], partner).wait_send()
    out_copy.wait()


def body(dims, density, passive, support, load_nodes, load_force, self_weight, body_force):
    loads, bricks, cells_x, size_y, size_z, nodes = dims
    local_loads = body_force.shape[0]
    rows_hi = loads // CORES
    zs = bricks // (XS * YLS)
    slab = size_y // loads
    ext = cells_x + 2 * HALO
    group_one, group_two = loads * YLS, zs * XS
    steps = DESIGN_ITERS
    layer = (size_y, size_z)
    padded = (size_y + 2 * PAD, size_z)
    vmem = pltpu.VMEM
    dma, regular = pltpu.SemaphoreType.DMA, pltpu.SemaphoreType.REGULAR
    space_any = pl.BlockSpec(memory_space=pl.ANY)
    space_vmem = pl.BlockSpec(memory_space=pltpu.VMEM)
    space_smem = pl.BlockSpec(memory_space=pltpu.SMEM)
    piece = (cells_x, slab, size_z)
    results = pl.pallas_call(
        functools.partial(kernel, dims),
        out_shape=(
            jax.ShapeDtypeStruct((cells_x, slab, size_z), F32),
            jax.ShapeDtypeStruct((cells_x, slab, size_z), F32),
            jax.ShapeDtypeStruct((local_loads, cells_x) + layer, F32),
        ),
        in_specs=[space_any, space_any, space_any, space_vmem, space_vmem, space_smem, space_any],
        out_specs=(space_vmem, space_vmem, space_any),
        scratch_shapes=[
            vmem((steps, ext) + layer, F32),
            vmem((ext,) + layer, jnp.int32),
            vmem((ext,) + layer, jnp.int32),
            vmem((local_loads, ext) + layer, F32),
            vmem((local_loads, ext) + layer, F32),
            vmem((ext,) + padded, F32),
            vmem((6, ext) + layer, F32),
            ((vmem((ext,) + padded, F32),) * (SWEEPS - 1),) * local_loads,
            vmem((local_loads, ext) + layer, F32),
            vmem((ext,) + padded, F32),
            vmem((local_loads, ext) + padded, F32),
            vmem((cells_x,) + layer, F32),
            vmem((steps, rows_hi) + piece, F32),
            vmem((steps, rows_hi) + piece, F32),
            vmem((steps, rows_hi) + piece, F32),
            vmem((ext,) + layer, F32),
            vmem((steps, 2, 8, size_z), F32),
            vmem((steps, group_one, 8, size_z), F32),
            vmem((steps, group_two, 8, size_z), F32),
            dma((4,)),
            dma((2,)), dma((2,)),
            dma((2,)), dma((2,)), dma((2,)), dma((2,)),
            dma((2,)), dma((2,)), dma((2,)), dma((2,)),
            dma((steps, rows_hi)), dma((steps, rows_hi)),
            dma((steps, rows_hi)), dma((steps, rows_hi)),
            dma((rows_hi,)), dma((rows_hi,)), dma((rows_hi,)), dma((rows_hi,)),
            dma((2,)), dma((2,)), dma((2,)), dma((2,)),
            dma((rows_hi, 2)), dma((rows_hi, 2)), dma((rows_hi, 2)), dma((rows_hi, 2)),
            dma((steps,)), dma((steps,)), dma((steps,)), dma((steps,)),
            dma,
            regular((2, 2, max(YLS * rows_hi, zs) // 2)), regular, regular,
        ],
        compiler_params=pltpu.CompilerParams(collective_id=0, has_side_effects=True),
    )(density, passive, support, load_nodes, load_force, self_weight, body_force)
    parts = [(0, slice(0, cells_x)), (1, slice(0, cells_x))]
    parts += [(2, one) for one in range(local_loads)]
    return pl.pallas_call(
        functools.partial(hand_over, parts),
        out_shape=tuple(jax.ShapeDtypeStruct(value.shape, value.dtype) for value in results),
        in_specs=[space_any] * 3,
        out_specs=(space_any,) * 3,
        scratch_shapes=[vmem(value.shape, F32) for value in results]
        + [dma((len(parts),)), dma((len(parts),))],
    )(*results)


def hand_over(parts, *refs):
    sources, targets, held, (come, go) = refs[0:3], refs[3:6], refs[6:9], refs[9:]
    into = [pltpu.make_async_copy(sources[i].at[at], held[i].at[at], come.at[n]) for n, (i, at) in enumerate(parts)]
    out = [pltpu.make_async_copy(held[i].at[at], targets[i].at[at], go.at[n]) for n, (i, at) in enumerate(parts)]
    for copy in into:
        copy.start()
    for first, second in zip(into, out):
        first.wait()
        second.start()
    for copy in out:
        copy.wait()


def solution(mesh):
    placed = (
        P("brick", None, None),
        P("brick", None, None),
        P("brick", None, None),
        P("load", None),
        P("load", None),
        P("load"),
        P("load", "brick", None, None),
    )

    def whole(*args):
        loads, bricks = mesh.shape["load"], mesh.shape["brick"]
        cells, size_y, size_z = args[0].shape
        dims = (loads, bricks, cells // bricks, size_y, size_z, args[3].shape[1])
        return jax.shard_map(
            functools.partial(body, dims),
            mesh=mesh,
            in_specs=placed,
            out_specs=(
                P("brick", "load", None),
                P("brick", "load", None),
                P("load", "brick", None, None),
            ),
            check_vma=False,
        )(*args)

    return whole
```

```python
import functools

import jax
import jax.numpy as jnp
from jax import lax
from jax.experimental import pallas as pl
from jax.experimental.pallas import tpu as pltpu
from jax.sharding import PartitionSpec as P

SWEEPS = 5
DESIGN_ITERS = 2
HALO = 7
WIDE = HALO - 1
PIECES = 4
PAD = 8
XS, YLS, CORES = 4, 2, 2

stiff_floor = 0.01
mass_shift = 0.1
spectrum_low = 0.05
spectrum_high = 2.0
moment_decay = 0.8
step_size = 0.1
volume_pull = 0.5
volume_target = 0.4
density_floor = 0.001

F32 = jnp.float32


def chebyshev_factors():
    centre = 0.5 * (spectrum_high + spectrum_low)
    half_width = 0.5 * (spectrum_high - spectrum_low)
    ratio_one = centre / half_width
    previous = 1.0 / ratio_one
    factors = []
    for _ in range(SWEEPS - 1):
        current = 1.0 / (2.0 * ratio_one - previous)
        factors.append((current * previous, 2.0 * current / half_width))
        previous = current
    return 1.0 / centre, factors


def passive_apply(design, passive):
    return jnp.where(passive == 1, density_floor, jnp.where(passive == 2, 1.0, design))


def kernel(
    dims,
    density_ref, passive_ref, support_ref, nodes_ref, force_ref, weight_ref, body_ref,
    new_ref, moment_ref, disp_ref,
    design, support, passive, source, points, stiff, coef, direct, resid, sens, moved_x,
    part, pair_in, pair_out, row_in, filt, msg, slots_one, slots_two,
    load_sems, body_send, body_recv, sup_send, sup_recv, supf_send, supf_recv,
    des_send, des_recv, desf_send, desf_recv,
    pair_send, pair_recv, row_send, row_recv, gath_send, gath_recv, gatf_send, gatf_recv,
    pas_send, pas_recv, pasf_send, pasf_recv, fil_send, fil_recv, filf_send, filf_recv,
    one_send, one_recv, two_send, two_recv, disp_sem, hello, column_in, partner_in,
):
    loads, bricks, cells_x, size_y, size_z, nodes = dims
    rows_hi = loads // CORES
    zs = bricks // (XS * YLS)
    slab = size_y // loads
    half = size_y // CORES
    ext = cells_x + 2 * HALO
    total_x = bricks * cells_x
    total_cells = float(total_x * size_y * size_z)
    last = HALO + cells_x
    local_loads = body_ref.shape[0]

    load = lax.axis_index("load")
    brick = lax.axis_index("brick")
    core = lax.rem(load, CORES)
    row = load // CORES
    at_x = lax.rem(brick, XS)
    at_yl = lax.rem(brick // XS, YLS)
    at_z = brick // (XS * YLS)
    has_low = brick > 0
    has_high = brick < bricks - 1
    partner = {"load": row * CORES + 1 - core, "brick": brick}

    def device(load_index, brick_index):
        return {"load": load_index, "brick": brick_index}

    group_one = rows_hi * YLS * CORES
    me_one = (row * YLS + at_yl) * CORES + core
    group_two = zs * XS
    me_two = at_z * XS + at_x

    def member_one(index):
        other_core = lax.rem(index, CORES)
        other_yl = lax.rem(index // CORES, YLS)
        other_row = index // (CORES * YLS)
        return device(other_row * CORES + other_core, (at_z * YLS + other_yl) * XS + at_x)

    def member_two(index):
        return device(load, (index // XS * YLS + at_yl) * XS + lax.rem(index, XS))

    def remote(src, dst, send, recv, target):
        return pltpu.make_async_remote_copy(
            src_ref=src, dst_ref=dst, send_sem=send, recv_sem=recv,
            device_id=target, device_id_type=pl.DeviceIdType.MESH,
        )

    own = pl.ds(HALO, cells_x)
    loads_in = [
        pltpu.make_async_copy(density_ref, design.at[0, own], load_sems.at[0]),
        pltpu.make_async_copy(passive_ref, passive.at[own], load_sems.at[1]),
        pltpu.make_async_copy(support_ref, support.at[own], load_sems.at[2]),
        pltpu.make_async_copy(body_ref, source.at[:, own], load_sems.at[3]),
    ]
    for copy in loads_in:
        copy.start()

    barrier = pltpu.get_barrier_semaphore()
    size_ring = {"y": YLS * rows_hi, "z": zs}

    def ring_peer(axis, shift):
        count = size_ring[axis]
        if axis == "z":
            there = lax.rem(at_z + shift + count, count)
            return device(load, (there * YLS + at_yl) * XS + at_x)
        there = lax.rem(row * YLS + at_yl + shift + count, count)
        return device(there // YLS * CORES + core, (at_z * YLS + lax.rem(there, YLS)) * XS + at_x)

    def x_peer(shift):
        return device(load, (at_z * YLS + at_yl) * XS + lax.rem(at_x + shift, XS))

    def signal(semaphore, target):
        pl.semaphore_signal(semaphore, 1, device_id=target, device_id_type=pl.DeviceIdType.MESH)

    @pl.when(has_low)
    def _():
        signal(barrier, device(load, brick - 1))

    @pl.when(has_high)
    def _():
        signal(barrier, device(load, brick + 1))

    signal(barrier, partner)
    for shift in range(1, XS):
        signal(barrier, x_peer(shift))
    for axis in ("y", "z"):
        for shift in (1, -1):
            signal(barrier, ring_peer(axis, shift))
    sides = jnp.where(has_low, 1, 0) + jnp.where(has_high, 1, 0)
    pl.semaphore_wait(barrier, 1 + (XS - 1) + 4 + sides)

    def pass_on(wave):
        for i, axis in enumerate(("y", "z")):
            waves = size_ring[axis] // 2 - 1
            for j, shift in enumerate((1, -1)):
                if 0 < wave <= waves:
                    pl.semaphore_wait(hello.at[i, j, wave - 1], 1)
                if wave < waves:
                    signal(hello.at[i, j, wave], ring_peer(axis, -shift))

    def rings_known():
        for shift in range(1, XS):
            signal(column_in, x_peer(shift))
        signal(partner_in, partner)

    low, high = device(load, brick - 1), device(load, brick + 1)
    mine = pl.ds(pl.multiple_of(core * half, half), half)
    others = pl.ds(pl.multiple_of((1 - core) * half, half), half)

    def halo_copies(src, src_first, dst, width, send, recv, lead, rows):
        cut = (lambda ref, first: ref.at[lead + (pl.ds(first, width),) + rows])
        down = remote(cut(src, src_first), cut(dst, last), send.at[0], recv.at[1], low)
        up = remote(cut(src, src_first + cells_x - width), cut(dst, HALO - width),
                    send.at[1], recv.at[0], high)
        return down, up

    def start_halo(copies):
        down, up = copies

        @pl.when(has_low)
        def _():
            down.start()

        @pl.when(has_high)
        def _():
            up.start()

    def landed(dst, width, recv, send, lead, rows, side):
        first = HALO - width if side == 0 else last
        ref = dst.at[lead + (pl.ds(first, width),) + rows]
        return remote(ref, ref, send.at[side], recv.at[side], partner)

    body_rows = (slice(None), slice(None))
    body_copies = [
        halo_copies(body_ref, 0, source, WIDE, body_send.at[one], body_recv.at[one], (one,), body_rows)
        for one in range(local_loads)
    ]
    sup_copies = halo_copies(support_ref, 0, support, WIDE, sup_send, sup_recv, (), (mine, slice(None)))
    start_halo(sup_copies)
    start_halo(body_copies[0])

    loads_in[0].wait()
    loads_in[1].wait()

    def first_design(layer, carry):
        design[0, layer + HALO] = passive_apply(design[0, layer + HALO], passive[layer + HALO])
        return carry

    lax.fori_loop(0, cells_x, first_design, 0)

    def clear(first):
        zero = jnp.zeros((size_y, size_z), F32)
        for layer in range(first, first + HALO):
            for step in range(DESIGN_ITERS):
                design[step, layer] = zero
            support[layer] = jnp.ones((size_y, size_z), jnp.int32)
            for one in range(local_loads):
                source[one, layer] = zero

    @pl.when(jnp.logical_not(has_low))
    def _():
        clear(0)

    @pl.when(jnp.logical_not(has_high))
    def _():
        clear(last)

    half_rows = (mine, slice(None))
    des_copies = halo_copies(design, HALO, design, HALO, des_send, des_recv, (0,), half_rows)
    start_halo(des_copies)
    for copies in body_copies[1:]:
        start_halo(copies)
    pas_copies = halo_copies(passive_ref, 0, passive, HALO, pas_send, pas_recv, (), half_rows)
    start_halo(pas_copies)
    pass_on(0)

    blank = jnp.zeros((PAD, size_z), F32)

    def clear_pads(layer, carry):
        for edge in (pl.ds(0, PAD), pl.ds(PAD + size_y, PAD)):
            stiff[layer, edge] = blank
            sens[layer, edge] = blank
            for one in range(local_loads):
                moved_x[one, layer, edge] = blank
                for k in range(SWEEPS - 1):
                    direct[one][k][layer, edge] = blank
        return carry

    lax.fori_loop(0, ext, clear_pads, 0)
    pass_on(1)
    loads_in[2].wait()
    loads_in[3].wait()

    node = nodes_ref[...]
    node_row = lax.shift_right_logical(node, size_z.bit_length() - 1)
    node_col = lax.bitwise_and(node, size_z - 1)
    flat_rows = jnp.concatenate([node_row[i:i + 1] for i in range(local_loads)], axis=1)
    flat_cols = jnp.concatenate([node_col[i:i + 1] for i in range(local_loads)], axis=1)
    flat_force = jnp.concatenate([force_ref[i:i + 1] for i in range(local_loads)], axis=1)
    width = local_loads * nodes
    col_of = jnp.transpose(jnp.broadcast_to(flat_cols.astype(F32), (size_z, width)))
    force_of = jnp.transpose(jnp.broadcast_to(flat_force, (size_z, width)))
    lanes = lax.broadcasted_iota(jnp.int32, (width, size_z), 1).astype(F32)
    owner = lax.broadcasted_iota(jnp.int32, (width, size_z), 0) // nodes
    placed = jnp.where(lanes == col_of, force_of, 0.0)
    spread = jnp.concatenate(
        [jnp.where(owner == i, placed, 0.0) for i in range(local_loads)], axis=1
    )
    batch = 4
    row_iota = lax.broadcasted_iota(jnp.int32, (batch * size_y, width), 0)

    def find_points(turn, carry):
        layer = turn * batch + HALO - WIDE
        base = (brick * cells_x + layer - HALO) * size_y
        hot = jnp.where(row_iota + base == flat_rows, 1.0, 0.0)
        found = jnp.dot(hot, spread, preferred_element_type=F32, precision=lax.Precision.HIGHEST)
        for i in range(batch):
            for one in range(local_loads):
                points[one, layer + i] = found[
                    i * size_y:(i + 1) * size_y, one * size_z:(one + 1) * size_z]
        return carry

    assert (cells_x + 2 * WIDE) % batch == 0
    lax.fori_loop(0, (cells_x + 2 * WIDE) // batch, find_points, 0)
    pass_on(2)

    iota_y = lax.broadcasted_iota(jnp.int32, (size_y, size_z), 0)
    iota_z = lax.broadcasted_iota(jnp.int32, (size_y, size_z), 1)
    y_first, y_last = iota_y == 0, iota_y == size_y - 1
    z_first, z_last = iota_z == 0, iota_z == size_z - 1
    piece_rows = size_y // PIECES
    rows_in = pl.ds(PAD, size_y)
    rows_next = pl.ds(PAD + 1, size_y)
    rows_back = pl.ds(PAD - 1, size_y)

    def z_up(value):
        return pltpu.roll(value, size_z - 1, 1)

    def z_down(value):
        return pltpu.roll(value, 1, 1)

    def z_sides(value):
        return jnp.where(z_last, 0.0, z_up(value)), jnp.where(z_first, 0.0, z_down(value))

    first_scale, factors = chebyshev_factors()

    def run(first, stop, body, most=4):
        count = stop - first
        group = max(n for n in range(1, most + 1) if count % n == 0)

        def turn(index, carry):
            for i in range(group):
                body(first + HALO + index * group + i)
            return carry

        lax.fori_loop(0, count // group, turn, 0)

    def make_stiff(step):
        def body(e):
            at = brick * cells_x + e - HALO
            inside = jnp.where(jnp.logical_and(at >= 0, at < total_x), 1.0, 0.0).astype(F32)
            value = design[step, e]
            stiff[e, rows_in] = inside * (stiff_floor + (1.0 - stiff_floor) * (value * value * value))
        return body

    def make_coef(step):
        def body(e):
            s = stiff[e, rows_in]
            free = (1 - support[e]).astype(F32)
            sides = (stiff[e + 1, rows_in], stiff[e - 1, rows_in],
                     stiff[e, rows_next], stiff[e, rows_back]) + z_sides(s)
            faces = [0.5 * (s + side) for side in sides]
            total = faces[0]
            for face in faces[1:]:
                total = total + face
            scale = free / (free * (total + mass_shift * s) + (1.0 - free))
            outer = (None, None, None, None, z_last, z_first)
            for j in range(6):
                value = scale * faces[j]
                coef[j, e] = value if outer[j] is None else jnp.where(outer[j], 0.0, value)
            here = design[step, e]
            for one in range(local_loads):
                force = source[one, e]
                if step == 0:
                    force = force + points[one, e]
                    source[one, e] = force
                start = scale * (force + weight_ref[one] * here)
                resid[one, e] = start
                direct[one][0][e, rows_in] = first_scale * start
        return body

    def make_sweep(k):
        keep, pull = factors[k]

        def body(e):
            for part_rows in range(0, size_y, piece_rows):
                inner = pl.ds(part_rows, piece_rows)
                here, below, above = (pl.ds(PAD + part_rows + shift, piece_rows) for shift in (0, 1, -1))
                c = [coef[j, e, inner] for j in range(6)]
                for one in range(local_loads):
                    level = direct[one][k]
                    d = level[e, here]
                    total = c[0] * level[e + 1, here] + c[1] * level[e - 1, here]
                    total = total + (c[2] * level[e, below] + c[3] * level[e, above])
                    total = total + (c[4] * z_up(d) + c[5] * z_down(d))
                    left = (resid[one, e, inner] - d) + total
                    if k < SWEEPS - 2:
                        resid[one, e, inner] = left
                        direct[one][k + 1][e, here] = keep * d + pull * left
                    else:
                        full = keep * d + pull * left + d
                        for older in range(k):
                            full = full + direct[one][older][e, here]
                        moved_x[one, e, here] = full
        return body

    def make_sens(step):
        def body(e):
            total = squares = up_gaps = None
            for one in range(local_loads):
                f = moved_x[one, e, rows_in]
                square = f * f
                gaps = None
                for beside in (moved_x[one, e + 1, rows_in], moved_x[one, e - 1, rows_in],
                               moved_x[one, e, rows_next], moved_x[one, e, rows_back]):
                    gap = f - beside
                    gaps = gap * gap if gaps is None else gaps + gap * gap
                gap = f - jnp.where(z_last, 0.0, z_up(f))
                gap = gap * gap
                value = mass_shift * square + 0.25 * (gaps + gap)
                total = value if total is None else total + value
                squares = square if squares is None else squares + square
                up_gaps = gap if up_gaps is None else up_gaps + gap
            total = total + 0.25 * jnp.where(z_first, squares, z_down(up_gaps))
            here = design[step, e]
            sens[e, rows_in] = (-3.0 * (1.0 - stiff_floor)) * (here * here) * total
        return body

    edge_count = (
        y_first.astype(F32) + y_last.astype(F32) + z_first.astype(F32) + z_last.astype(F32)
    )

    def filter_layer(e):
        at = brick * cells_x + e - HALO
        end = jnp.where(jnp.logical_or(at == 0, at == total_x - 1), 1.0, 0.0).astype(F32)
        value = sens[e, rows_in]
        total = 2.0 * value + sens[e + 1, rows_in] + sens[e - 1, rows_in]
        total = total + sens[e, rows_next] + sens[e, rows_back]
        for beside in z_sides(value):
            total = total + beside
        part[e - HALO] = total / (8.0 - (edge_count + end))

    def slab_rows(index):
        return pl.ds(pl.multiple_of(index * slab, slab), slab)

    def other_row(k):
        return lax.rem(row + k, rows_hi)

    my_slab = slab_rows(load)

    both_sides = ((0, has_low), (1, has_high))

    def to_partner(ref, lead, width, side, send, recv, rows):
        first = HALO - width if side == 0 else last
        ref = ref.at[lead + (pl.ds(first, width), rows)]
        return remote(ref, ref, send, recv, partner)

    def pass_to_partner(ref, lead, width, side, near, far):
        landed(ref, width, near[1], near[0], lead, half_rows, side).wait_recv()
        to_partner(ref, lead, width, side, far[0].at[side], far[1].at[side], mine).start()

    sup_sems, des_sems, pas_sems = (
        ((sup_send, sup_recv), (supf_send, supf_recv)),
        ((des_send, des_recv), (desf_send, desf_recv)),
        ((pas_send, pas_recv), (pasf_send, pasf_recv)),
    )
    halo_kinds = ((support, (), WIDE, sup_sems), (design, (0,), HALO, des_sems), (passive, (), HALO, pas_sems))

    def came_from_partner(kind, side):
        ref, lead, width, sems = kind
        to_partner(ref, lead, width, side, sems[1][0].at[side], sems[1][1].at[side], others).wait_recv()

    def pass_filtered(k):
        rows = slab_rows(lax.rem(row + rows_hi - k, rows_hi) * CORES + core)
        down = remote(filt.at[pl.ds(HALO, HALO), rows], filt.at[pl.ds(last, HALO), rows],
                      fil_send.at[k, 0], fil_recv.at[k, 1], low)
        up = remote(filt.at[pl.ds(cells_x, HALO), rows], filt.at[pl.ds(0, HALO), rows],
                    fil_send.at[k, 1], fil_recv.at[k, 0], high)
        return down, up

    def filtered_halo(k, side, whose):
        index = lax.rem(row + rows_hi - k, rows_hi) * CORES + whose
        return filt.at[pl.ds(0 if side == 0 else last, HALO), slab_rows(index)]

    cut = (cells_x - 2) // 2
    pieces = (pl.ds(0, cut), pl.ds(cut, cells_x - cut))
    order = sorted(range(1, rows_hi), key=lambda k: -min(k, rows_hi - k)) + [0]
    to_pair = [[] for _ in range(DESIGN_ITERS)]
    to_row = [[] for _ in range(DESIGN_ITERS)]

    def pair_copy(step, piece, k, rows):
        at, index = pieces[piece], other_row(k)
        return remote(part.at[at, rows], pair_in.at[step, index, at], pair_send.at[step, piece, k],
                      pair_recv.at[step, piece, index], partner)

    def pair_piece(step, piece):
        for k in order:
            copy = pair_copy(step, piece, k, slab_rows(other_row(k) * CORES + 1 - core))
            copy.start()
            to_pair[step].append(copy)

    def row_piece(step, piece):
        at = pieces[piece]
        for k in order:
            index = other_row(k)
            rows = slab_rows(index * CORES + core)
            pair_copy(step, piece, k, rows).wait_recv()
            pair_out[step, k, at] = part[at, rows] + pair_in[step, index, at]
            if k:
                copy = remote(pair_out.at[step, k, at], row_in.at[step, k, at], row_send.at[step, piece, k],
                              row_recv.at[step, piece, k], device(index * CORES + core, brick))
                copy.start()
                to_row[step].append(copy)

    for step in range(DESIGN_ITERS):
        final = step == DESIGN_ITERS - 1
        if step == 0:
            run(0, cells_x, make_stiff(step))
            run(1, cells_x - 1, make_coef(step), 5)
            pass_on(3)
            rings_known()
            for k in range(SWEEPS - 1):
                run(2 + k, cells_x - 2 - k, make_sweep(k))

            for side, there in both_sides:
                @pl.when(there)
                def _(side=side):
                    for ref, lead, width, (near, far) in halo_kinds[:2]:
                        pass_to_partner(ref, lead, width, side, near, far)

            for side, there in both_sides:
                @pl.when(there)
                def _(side=side):
                    for one in range(local_loads):
                        landed(source, WIDE, body_recv.at[one], body_send.at[one], (one,), body_rows, side).wait_recv()
                    for kind in halo_kinds[:2]:
                        came_from_partner(kind, side)

                low_end = (lambda a, b: (a, b)) if side == 0 else (lambda a, b: (cells_x - b, cells_x - a))
                run(*low_end(-HALO, 0), make_stiff(step))
                run(*low_end(-WIDE, 1), make_coef(step), 7)
                if side == 1:
                    pl.semaphore_wait(column_in, XS - 1)
                    pl.semaphore_wait(partner_in, 1)
                    row_piece(step, 0)
                for k in range(SWEEPS - 1):
                    run(*low_end(k + 1 - WIDE, 2 + k), make_sweep(k), 7)
                if side == 0:
                    run(-1, cut + 1, make_sens(step), 7)
                    run(0, cut, filter_layer, 7)
                    pair_piece(step, 0)

            for side, there in both_sides:
                @pl.when(there)
                def _(side=side):
                    ref, lead, width, (near, far) = halo_kinds[2]
                    pass_to_partner(ref, lead, width, side, near, far)
        else:
            run(-HALO, cells_x + HALO, make_stiff(step))
            run(-WIDE, cells_x + WIDE, make_coef(step))
            for k in range(SWEEPS - 1):
                run(k + 1 - WIDE, cells_x + WIDE - 1 - k, make_sweep(k), 5)
        if final:
            out_copy = pltpu.make_async_copy(moved_x.at[:, own, rows_in], disp_ref, disp_sem)
            out_copy.start()
        if step:
            run(-1, cut + 1, make_sens(step), 7)
            run(0, cut, filter_layer, 7)
            pair_piece(step, 0)
        run(cut + 1, cells_x + 1, make_sens(step), 7)
        if step:
            row_piece(step, 0)
        run(cut, cells_x, filter_layer, 7)
        pair_piece(step, 1)
        row_piece(step, 1)
        total = pair_out[step, 0]
        for copy in to_row[step]:
            copy.wait_recv()
        for k in order[:-1]:
            total = total + row_in[step, k]
        if final:
            total = moment_decay * filt[own, my_slab] + total
            moment_ref[...] = total
        else:
            filt[own, my_slab] = total

        here = design[step, own, my_slab]

        def fold(value):
            value = jnp.sum(jnp.sum(value, axis=0), axis=0, keepdims=True)
            return value + pltpu.roll(value, size_z // 2, 1)

        left_half = lax.broadcasted_iota(jnp.int32, (1, size_z), 1) < size_z // 2
        message = jnp.where(left_half, fold(jnp.abs(total)), fold(here))

        def share(message, stage, slots, send, recv, me, count, member):
            first_row = pl.ds(0, 1)
            msg[step, stage, first_row] = message
            slots[step, me, first_row] = message
            for k in range(1, count):
                remote(msg.at[step, stage, first_row], slots.at[step, me, first_row], send.at[step],
                       recv.at[step], member(lax.rem(me + k, count))).start()

            def finish():
                ref = slots.at[step, pl.ds(0, count - 1), first_row]
                remote(ref, ref, send.at[step], recv.at[step], partner).wait_recv()
                return jnp.sum(slots[step, :, first_row], axis=0)

            def drain():
                ref = slots.at[step, pl.ds(0, count - 1), first_row]
                remote(ref, ref, send.at[step], recv.at[step], partner).wait_send()

            return finish, drain

        finish_one, drain_one = share(message, 0, slots_one, one_send, one_recv, me_one, group_one, member_one)

        gathers = []
        if not final:
            for k in order[:-1]:
                index = other_row(k)
                copy = remote(filt.at[own, my_slab], filt.at[own, my_slab], gath_send.at[k],
                              gath_recv.at[k], device(index * CORES + core, brick))
                copy.start()
                gathers.append(copy)
            start_halo(pass_filtered(0))
            copy = remote(filt.at[own, my_slab], filt.at[own, my_slab], gatf_send.at[0],
                          gatf_recv.at[0], partner)
            copy.start()
            gathers.append(copy)

        finish_two, drain_two = share(finish_one(), 1, slots_two, two_send, two_recv, me_two, group_two, member_two)

        if not final:
            for k in order[:-1][::-1]:
                index = lax.rem(row + rows_hi - k, rows_hi)
                ref = filt.at[own, slab_rows(index * CORES + core)]
                remote(ref, ref, gath_send.at[k], gath_recv.at[k], partner).wait_recv()
                start_halo(pass_filtered(k))
                copy = remote(ref, ref, gatf_send.at[k], gatf_recv.at[k], partner)
                copy.start()
                gathers.append(copy)
            came_in = [0] + order[:-1][::-1]
            for k in came_in:
                for side, there in both_sides:
                    @pl.when(there)
                    def _(k=k, side=side):
                        ref = filtered_halo(k, side, core)
                        remote(ref, ref, fil_send.at[k, side], fil_recv.at[k, side], partner).wait_recv()
                        remote(ref, ref, filf_send.at[k, side], filf_recv.at[k, side], partner).start()
            for k in came_in:
                index = lax.rem(row + rows_hi - k, rows_hi)
                ref = filt.at[own, slab_rows(index * CORES + 1 - core)]
                remote(ref, ref, gatf_send.at[k], gatf_recv.at[k], partner).wait_recv()
                for side, there in both_sides:
                    @pl.when(there)
                    def _(k=k, side=side):
                        ref = filtered_halo(k, side, 1 - core)
                        remote(ref, ref, filf_send.at[k, side], filf_recv.at[k, side], partner).wait_recv()
            for side, there in both_sides:
                @pl.when(there)
                def _(side=side):
                    came_from_partner(halo_kinds[2], side)

        sums = finish_two()
        abs_total = jnp.sum(jnp.where(left_half, sums, 0.0), keepdims=True)
        density_total = jnp.sum(jnp.where(left_half, 0.0, sums), keepdims=True)
        rate = step_size / (abs_total / total_cells + 1e-06)
        pull_down = volume_pull * (density_total / total_cells - volume_target)

        def updated(old, moment, kind):
            value = old - rate * moment - pull_down
            return passive_apply(jnp.clip(value, density_floor, 1.0), kind)

        if final:
            def last_design(layer, carry):
                new_ref[layer] = updated(design[step, layer + HALO, my_slab],
                                         moment_ref[layer], passive[layer + HALO, my_slab])
                return carry

            lax.fori_loop(0, cells_x, last_design, 0)
        else:
            def next_design(e):
                design[step + 1, e] = updated(design[step, e], filt[e], passive[e])

            @pl.when(has_low)
            def _():
                run(-HALO, 0, next_design, 7)

            run(0, cells_x, next_design, 6)

            @pl.when(has_high)
            def _():
                run(cells_x, cells_x + HALO, next_design, 7)

        for copy in to_pair[step] + to_row[step] + gathers:
            copy.wait_send()
        drain_one()
        drain_two()

    for side, there in both_sides:
        @pl.when(there)
        def _(side=side):
            for copies in body_copies + [sup_copies, des_copies, pas_copies]:
                copies[side].wait_send()
            for ref, lead, width, sems in halo_kinds:
                to_partner(ref, lead, width, side, sems[1][0].at[side], sems[1][1].at[side], mine).wait_send()
            for k in range(rows_hi):
                pass_filtered(k)[side].wait_send()
                ref = filtered_halo(k, side, core)
                remote(ref, ref, filf_send.at[k, side], filf_recv.at[k, side], partner).wait_send()
    out_copy.wait()


def body(dims, density, passive, support, load_nodes, load_force, self_weight, body_force):
    loads, bricks, cells_x, size_y, size_z, nodes = dims
    local_loads = body_force.shape[0]
    rows_hi = loads // CORES
    zs = bricks // (XS * YLS)
    slab = size_y // loads
    ext = cells_x + 2 * HALO
    group_one, group_two = loads * YLS, zs * XS
    steps = DESIGN_ITERS
    layer = (size_y, size_z)
    padded = (size_y + 2 * PAD, size_z)
    vmem = pltpu.VMEM
    dma, regular = pltpu.SemaphoreType.DMA, pltpu.SemaphoreType.REGULAR
    space_any = pl.BlockSpec(memory_space=pl.ANY)
    space_vmem = pl.BlockSpec(memory_space=pltpu.VMEM)
    space_smem = pl.BlockSpec(memory_space=pltpu.SMEM)
    piece = (cells_x, slab, size_z)
    results = pl.pallas_call(
        functools.partial(kernel, dims),
        out_shape=(
            jax.ShapeDtypeStruct((cells_x, slab, size_z), F32),
            jax.ShapeDtypeStruct((cells_x, slab, size_z), F32),
            jax.ShapeDtypeStruct((local_loads, cells_x) + layer, F32),
        ),
        in_specs=[space_any, space_any, space_any, space_vmem, space_vmem, space_smem, space_any],
        out_specs=(space_vmem, space_vmem, space_any),
        scratch_shapes=[
            vmem((steps, ext) + layer, F32),
            vmem((ext,) + layer, jnp.int32),
            vmem((ext,) + layer, jnp.int32),
            vmem((local_loads, ext) + layer, F32),
            vmem((local_loads, ext) + layer, F32),
            vmem((ext,) + padded, F32),
            vmem((6, ext) + layer, F32),
            ((vmem((ext,) + padded, F32),) * (SWEEPS - 1),) * local_loads,
            vmem((local_loads, ext) + layer, F32),
            vmem((ext,) + padded, F32),
            vmem((local_loads, ext) + padded, F32),
            vmem((cells_x,) + layer, F32),
            vmem((steps, rows_hi) + piece, F32),
            vmem((steps, rows_hi) + piece, F32),
            vmem((steps, rows_hi) + piece, F32),
            vmem((ext,) + layer, F32),
            vmem((steps, 2, 8, size_z), F32),
            vmem((steps, group_one, 8, size_z), F32),
            vmem((steps, group_two, 8, size_z), F32),
            dma((4,)),
            dma((local_loads, 2)), dma((local_loads, 2)),
            dma((2,)), dma((2,)), dma((2,)), dma((2,)),
            dma((2,)), dma((2,)), dma((2,)), dma((2,)),
            dma((steps, 2, rows_hi)), dma((steps, 2, rows_hi)),
            dma((steps, 2, rows_hi)), dma((steps, 2, rows_hi)),
            dma((rows_hi,)), dma((rows_hi,)), dma((rows_hi,)), dma((rows_hi,)),
            dma((2,)), dma((2,)), dma((2,)), dma((2,)),
            dma((rows_hi, 2)), dma((rows_hi, 2)), dma((rows_hi, 2)), dma((rows_hi, 2)),
            dma((steps,)), dma((steps,)), dma((steps,)), dma((steps,)),
            dma,
            regular((2, 2, max(YLS * rows_hi, zs) // 2)), regular, regular,
        ],
        compiler_params=pltpu.CompilerParams(collective_id=0, has_side_effects=True),
    )(density, passive, support, load_nodes, load_force, self_weight, body_force)
    parts = [(0, slice(0, cells_x)), (1, slice(0, cells_x))]
    parts += [(2, one) for one in range(local_loads)]
    return pl.pallas_call(
        functools.partial(hand_over, parts),
        out_shape=tuple(jax.ShapeDtypeStruct(value.shape, value.dtype) for value in results),
        in_specs=[space_any] * 3,
        out_specs=(space_any,) * 3,
        scratch_shapes=[vmem(value.shape, F32) for value in results]
        + [dma((len(parts),)), dma((len(parts),))],
    )(*results)


def hand_over(parts, *refs):
    sources, targets, held, (come, go) = refs[0:3], refs[3:6], refs[6:9], refs[9:]
    into = [pltpu.make_async_copy(sources[i].at[at], held[i].at[at], come.at[n]) for n, (i, at) in enumerate(parts)]
    out = [pltpu.make_async_copy(held[i].at[at], targets[i].at[at], go.at[n]) for n, (i, at) in enumerate(parts)]
    for copy in into:
        copy.start()
    for first, second in zip(into, out):
        first.wait()
        second.start()
    for copy in out:
        copy.wait()


def solution(mesh):
    placed = (
        P("brick", None, None),
        P("brick", None, None),
        P("brick", None, None),
        P("load", None),
        P("load", None),
        P("load"),
        P("load", "brick", None, None),
    )

    def whole(*args):
        loads, bricks = mesh.shape["load"], mesh.shape["brick"]
        cells, size_y, size_z = args[0].shape
        dims = (loads, bricks, cells // bricks, size_y, size_z, args[3].shape[1])
        return jax.shard_map(
            functools.partial(body, dims),
            mesh=mesh,
            in_specs=placed,
            out_specs=(
                P("brick", "load", None),
                P("brick", "load", None),
                P("load", "brick", None, None),
            ),
            check_vma=False,
        )(*args)

    return whole
```
